768 devices in a mesh: row: 24 (over z_lo, x), col: 8 (over y), rep: 4 (over z_hi, core).
Axes of the slice: x: 4, y: 8, z: 12 (z_hi: 2, z_lo: 6; z = z_hi * 6 + z_lo), core: 2. Of those that a mesh axis runs over, the one named last changes fastest.
Arguments:
- vectors: float32 [8, 24576], P('rep', ('row', 'col')), may hold values from -6 to 6
- energies: float32 [24576], P(('row', 'col')), may hold values from 0 to 16
- tiles: bfloat16 [11520, 128, 128], P(('row', 'col', 'rep')), may hold values from -0.078125 to 0.078125
- tile_codes: int32 [11520], P(('row', 'col', 'rep')), may hold values from -1 to 191, as said below
Outputs:
- filtered: float32 [8, 24576], P('rep', ('row', 'col'))
- ritz_values: float32 [8], P('rep')
The draws below stay inside these ranges and needn't reach their ends.
Inputs may be any that keep to these rules, and one draw needn't show every extreme that they name: `tile_codes`: slots of device (row, col, rep) hold tiles of grid cell (row, col) only. A code q stands for block row row * 8 + q // 24 and block column (q % 24) * 8 + col, which lies on or above the diagonal. Each cell holds its diagonal tile, each position at most once; a cell's tiles, in increasing code order, are dealt to its 4 devices in turn, so the occupied slots of a device come first and the rest are -1. Some device fills all 15 slots.
All inputs are finite; a program needn't handle non-finite values.
Results may differ from the reference program's by a relative error of at most 0.002.
Values may be sent and summed in bfloat16 or wider, within the bound.
No kernel may reach another device: no remote copies, remote signals or barrier semaphores. Data moves between devices by JAX's collectives and lax.ppermute only.
A program may use at most 32 MiB of HBM per device.

```python
import jax
import jax.numpy as jnp
from jax import lax

TILE = 128
NV = 8
OUTER = 1
PASSES = 1
DEG = 2
NR = 24
NC = 8
NP = 4
NB = 192
NS = 24576
SLOTS = 15


def tile_layout(key):
    cell_total = NR * NC
    cells = jnp.arange(cell_total, dtype=jnp.int32)
    cell_row = cells // NC
    cell_col = cells % NC
    spots = jnp.arange(NB, dtype=jnp.int32)
    block_i = cell_row[:, None] * NC + (spots // NR)[None, :]
    block_j = (spots % NR)[None, :] * NC + cell_col[:, None]
    upper = block_j >= block_i
    diagonal = block_j == block_i
    corner = (cells == NC - 1)[:, None] & (spots == NB - 1)[None, :]
    forced = diagonal | corner
    upper_count = jnp.sum(upper, axis=1).astype(jnp.int32)
    forced_count = jnp.sum(forced, axis=1).astype(jnp.int32)
    density = jax.random.randint(jax.random.fold_in(key, 101), (cell_total,), 80, 301)
    density = jnp.where(cells == NC - 1, 300, density)
    floor_count = jax.random.randint(jax.random.fold_in(key, 303), (cell_total,), 1, 3)
    counts = jnp.maximum(floor_count, density * upper_count // 1000)
    counts = jnp.minimum(counts, jnp.minimum(upper_count, NP * SLOTS))
    counts = jnp.maximum(counts, forced_count)
    subkeys = jax.random.split(jax.random.fold_in(key, 202), cell_total)
    ranks = jax.vmap(lambda subkey: jax.random.permutation(subkey, NB))(subkeys).astype(jnp.int32)
    scores = jnp.where(diagonal, 5 * NB + spots[None, :], jnp.where(forced, 3 * NB + spots[None, :], jnp.where(upper, NB + ranks, -1 - spots[None, :])))
    order = jnp.argsort(-scores, axis=1, stable=True)
    places = jnp.argsort(order, axis=1, stable=True)
    chosen = places < counts[:, None]
    ordered = jnp.sort(jnp.where(chosen, spots[None, :], NB + spots[None, :]), axis=1)
    turns = jnp.arange(SLOTS, dtype=jnp.int32)[None, :] * NP + jnp.arange(NP, dtype=jnp.int32)[:, None]
    picked = ordered[:, jnp.minimum(turns, NB - 1)]
    codes = jnp.where(turns[None, :, :] < counts[:, None, None], picked, -1)
    return codes.reshape(-1).astype(jnp.int32)


def draw_tile_codes(key, part):
    return tile_layout(key)


def levels(key, shape, cuts, low, high):
    gain = 1.0
    for axis_at, parts in cuts:
        draws = jax.random.uniform(jax.random.fold_in(jax.random.fold_in(key, 6), axis_at), (parts,), jnp.float32, low / len(cuts), high / len(cuts))
        gain = gain * jnp.repeat(jnp.exp(draws), shape[axis_at] // parts).reshape((-1,) + (1,) * (len(shape) - 1 - axis_at))
    return gain


def bell_draw(stream_key, extent, width, bound, shards=(), held_as=jnp.bfloat16):
    drawn = jax.random.normal(stream_key, extent, jnp.float32) * width
    if len(shards) > 0:
        drawn = levels(stream_key, extent, shards, -0.22, 0.18) * drawn
    return jnp.clip(drawn, min=-bound, max=bound).astype(held_as)


def setup_inputs(seed: int = 0) -> dict:
    key_of = jax.random.split(jax.random.key(seed), 5)
    vectors = bell_draw(key_of[0], (NV, NS), 1.0, 6.0, ((0, 4), (1, 192)), jnp.float32)
    energies = jnp.clip(16.0 * jax.random.uniform(key_of[1], (NS,), jnp.float32) ** levels(key_of[1], (NS,), ((0, 192),), -0.2, 0.2), 0.0, 16.0)
    tiles = bell_draw(key_of[2], (NR * NC * NP * SLOTS, TILE, TILE), (TILE * NB // 4) ** -0.5, 0.078125, ((0, 768),))
    tile_codes = draw_tile_codes(jax.random.fold_in(key_of[4], 71), 0)
    return {"vectors": vectors, "energies": energies, "tiles": tiles, "tile_codes": tile_codes}


filter_low = 5.0
filter_top = 20.0
spectrum_low = -3.0


def reference(vectors, energies, tiles, tile_codes):
    slot_count = tiles.shape[0]
    tile_side = tiles.shape[1]
    cell_index = jnp.arange(slot_count, dtype=jnp.int32) // (NP * SLOTS)
    cell_row = cell_index // NC
    cell_col = cell_index % NC
    present = tile_codes >= 0
    safe_code = jnp.where(present, tile_codes, 0).astype(jnp.int32)
    block_i = (cell_row * NC + safe_code // NR).astype(jnp.int32)
    block_j = ((safe_code % NR) * NC + cell_col).astype(jnp.int32)
    upper_mask = lax.broadcasted_iota(jnp.int32, (tile_side, tile_side), 1) > lax.broadcasted_iota(jnp.int32, (tile_side, tile_side), 0)
    keep_mask = present[:, None, None] & (upper_mask[None] | (block_i != block_j)[:, None, None])
    stored = jnp.where(keep_mask, tiles, jnp.zeros((), tiles.dtype)).astype(jnp.float32)

    def product(vector_block):
        rounded = lax.optimization_barrier(vector_block.astype(jnp.bfloat16)).astype(jnp.float32)
        rounded = rounded.reshape(NV, NB, TILE)
        direct = jnp.einsum("vsj,sij->svi", rounded[:, block_j], stored, precision=lax.Precision.HIGHEST)
        mirror = jnp.einsum("vsi,sij->svj", rounded[:, block_i], stored, precision=lax.Precision.HIGHEST)
        total = jnp.zeros((NB, NV, TILE), jnp.float32).at[block_i].add(direct).at[block_j].add(mirror)
        return energies[None, :] * vector_block + jnp.transpose(total, (1, 0, 2)).reshape(NV, NS)

    half = (filter_top - filter_low) / 2.0
    centre = (filter_top + filter_low) / 2.0
    sigma_first = half / (spectrum_low - centre)
    tau_value = 2.0 / sigma_first
    current = vectors
    ritz = jnp.zeros((NV,), jnp.float32)
    for outer_step in range(OUTER):
        for pass_step in range(PASSES):
            previous = current
            latest = (product(current) - centre * current) * (sigma_first / half)
            sigma_now = sigma_first
            for degree_step in range(1, DEG):
                sigma_next = 1.0 / (tau_value - sigma_now)
                newest = (product(latest) - centre * latest) * (2.0 * sigma_next / half) - (sigma_now * sigma_next) * previous
                previous = latest
                latest = newest
                sigma_now = sigma_next
            current = latest
        image = product(current)
        squares = jnp.sum(current * current, axis=1)
        crossed = jnp.sum(current * image, axis=1)
        ritz = crossed / (squares + 1e-6)
        resid = image - ritz[:, None] * current
        spacing = energies[None, :] - ritz[:, None]
        current = current - spacing / jnp.maximum(spacing * spacing, 1.0) * resid
    return current, ritz
```

```python
import functools

import jax
import jax.numpy as jnp
from jax import lax
from jax.experimental import pallas as pl
from jax.experimental.pallas import tpu as pltpu
from jax.sharding import Mesh
from jax.sharding import PartitionSpec as P

ROW = ("z_lo", "x")
REP = ("z_hi", "core")
ROW_COL = ("z_lo", "x", "col")
ROW_COL_REP = ("z_lo", "x", "col", "z_hi", "core")

filter_low = 5.0
filter_top = 20.0
spectrum_low = -3.0

half = (filter_top - filter_low) / 2.0
centre = (filter_top + filter_low) / 2.0
sigma_first = half / (spectrum_low - centre)
tau_value = 2.0 / sigma_first
sigma_next = 1.0 / (tau_value - sigma_first)

VMEM = pl.BlockSpec(memory_space=pltpu.VMEM)
SMEM = pl.BlockSpec(memory_space=pltpu.SMEM)


def exchange(blocks, axis):
    return lax.all_to_all(blocks, axis, 0, 0, tiled=True)


def call(body, out_shapes, scalars, arrays, scratch):
    outs = [jax.ShapeDtypeStruct(shape, jnp.float32) for shape in out_shapes]
    return pl.pallas_call(
        body,
        out_shape=outs,
        in_specs=[SMEM] * len(scalars) + [VMEM] * len(arrays),
        out_specs=[VMEM] * len(outs),
        scratch_shapes=[pltpu.VMEM(shape, jnp.float32) for shape in scratch],
    )(*scalars, *arrays)


def mirror_products(table, x_ref, tile_refs, send_ref, me):
    rows, vecs = send_ref.shape[0], x_ref.shape[1]
    slots = tile_refs[0].shape[0]
    own = x_ref[me]
    for k in range(rows):
        send_ref[k, :vecs, :] = jnp.zeros_like(own)
        send_ref[k, vecs:, :] = own
    for group, tiles in enumerate(tile_refs):
        for slot in range(slots):
            a, k = table[0, group * slots + slot], table[1, group * slots + slot]
            part = lax.dot_general(
                x_ref[a].astype(jnp.bfloat16),
                tiles[slot],
                (((1,), (0,)), ((), ())),
                preferred_element_type=jnp.float32,
            )
            send_ref[k, :vecs, :] += part


def direct_products(table, got_ref, tile_refs, sums_ref):
    vecs = sums_ref.shape[1]
    slots = tile_refs[0].shape[0]
    sums_ref[...] = jnp.zeros_like(sums_ref)
    for group, tiles in enumerate(tile_refs):
        for slot in range(slots):
            a, k = table[0, group * slots + slot], table[1, group * slots + slot]
            part = lax.dot_general(
                got_ref[k, vecs:, :].astype(jnp.bfloat16),
                tiles[slot],
                (((1,), (1,)), ((), ())),
                preferred_element_type=jnp.float32,
            )
            sums_ref[a] += part


def summed_mirror(got_ref, vecs):
    total = got_ref[0, :vecs, :]
    for k in range(1, got_ref.shape[0]):
        total = total + got_ref[k, :vecs, :]
    return total


def start_kernel(table, me, first_ref, t0, t1, t2, t3, send_ref, x_ref):
    cols = first_ref.shape[0]
    vecs = x_ref.shape[1]
    for a in range(cols):
        x_ref[a] = first_ref[a, :vecs, :]
    mirror_products(table, x_ref, (t0, t1, t2, t3), send_ref, me[0])


def product_rows(got_ref, a):
    cols = got_ref.shape[0]
    total = got_ref[a, cols]
    for c in range(cols):
        total = total + got_ref[c, a]
    return total


def second_kernel(table, me, first_ref, got_ref, t0, t1, t2, t3, send_ref, x_ref):
    cols = first_ref.shape[0]
    vecs = x_ref.shape[1]
    for a in range(cols):
        x = first_ref[a, :vecs, :]
        energy = first_ref[a, vecs:, :]
        image = energy * x + product_rows(got_ref, a)
        x_ref[a] = (image - centre * x) * (sigma_first / half)
    mirror_products(table, x_ref, (t0, t1, t2, t3), send_ref, me[0])


def third_kernel(table, me, first_ref, last_ref, got_ref, t0, t1, t2, t3, send_ref, x_ref):
    cols = first_ref.shape[0]
    vecs = x_ref.shape[1]
    for a in range(cols):
        x = last_ref[a]
        energy = first_ref[a, vecs:, :]
        image = energy * x + product_rows(got_ref, a)
        x_ref[a] = (image - centre * x) * (2.0 * sigma_next / half) - (
            sigma_first * sigma_next
        ) * first_ref[a, :vecs, :]
    mirror_products(table, x_ref, (t0, t1, t2, t3), send_ref, me[0])


def direct_kernel(table, got_ref, t0, t1, t2, t3, send_ref, sums_ref):
    direct_products(table, got_ref, (t0, t1, t2, t3), sums_ref)
    cols, vecs = sums_ref.shape[0], sums_ref.shape[1]
    mirror = summed_mirror(got_ref, vecs)
    for c in range(cols):
        for a in range(cols):
            send_ref[c, a] = sums_ref[a]
        send_ref[c, cols] = mirror


def last_direct_kernel(table, me, first_ref, x_ref, got_ref, t0, t1, t2, t3, send_ref, image_ref, sums_ref):
    direct_products(table, got_ref, (t0, t1, t2, t3), sums_ref)
    cols, vecs = sums_ref.shape[0], sums_ref.shape[1]
    x = x_ref[me[0]]
    image = first_ref[me[0], vecs:, :] * x + summed_mirror(got_ref, vecs)
    image_ref[...] = image
    crossed = x * image
    for a in range(cols):
        crossed = crossed + x_ref[a] * sums_ref[a]
    for c in range(cols):
        send_ref[c, 0] = sums_ref[c]
        send_ref[c, 1] = crossed
        send_ref[c, 2] = x * x


def image_kernel(part_ref, got_ref, image_ref, send_ref):
    cols = got_ref.shape[0]
    totals = [got_ref[0, i] for i in range(3)]
    for c in range(1, cols):
        totals = [total + got_ref[c, i] for i, total in enumerate(totals)]
    image_ref[...] = part_ref[...] + totals[0]
    for k in range(send_ref.shape[0]):
        send_ref[k, 0] = totals[1]
        send_ref[k, 1] = totals[2]


def correct_kernel(me, first_ref, x_all_ref, image_ref, got_ref, out_ref, ritz_ref):
    crossed, squares = got_ref[0, 0], got_ref[0, 1]
    for k in range(1, got_ref.shape[0]):
        crossed = crossed + got_ref[k, 0]
        squares = squares + got_ref[k, 1]
    ritz = jnp.sum(crossed, axis=1, keepdims=True) / (
        jnp.sum(squares, axis=1, keepdims=True) + 1e-06
    )
    x = x_all_ref[me[0]]
    vecs = x.shape[0]
    resid = image_ref[...] - ritz * x
    spacing = first_ref[me[0], vecs:, :] - ritz
    out_ref[...] = x - spacing / jnp.maximum(spacing * spacing, 1.0) * resid
    ritz_ref[...] = jnp.broadcast_to(ritz, ritz_ref.shape)


def on_device(vectors, energies, tiles, tile_codes):
    rows = lax.axis_size(ROW)
    cols = lax.axis_size("col")
    reps = lax.axis_size(REP)
    cores = lax.axis_size("core")
    row_index = lax.axis_index(ROW)
    col_index = lax.axis_index("col")
    rep_index = lax.axis_index(REP)
    slots, side = tiles.shape[0], tiles.shape[1]
    vecs = vectors.shape[0]
    present = tile_codes >= 0
    safe_code = jnp.where(present, tile_codes, 0)
    on_diagonal = present & (safe_code == col_index * rows + row_index)
    upper_mask = lax.broadcasted_iota(jnp.int32, (side, side), 1) > lax.broadcasted_iota(
        jnp.int32, (side, side), 0
    )
    keep_mask = present[:, None, None] & (
        upper_mask[None] | jnp.logical_not(on_diagonal)[:, None, None]
    )
    stored = jnp.where(keep_mask, tiles, jnp.zeros((), tiles.dtype))
    far = lax.ppermute(stored, "z_hi", [(0, 1), (1, 0)])
    near = lax.ppermute(stored, "core", [(0, 1), (1, 0)])
    far_near = lax.ppermute(far, "core", [(0, 1), (1, 0)])
    groups = (stored, near, far, far_near)

    first = jnp.concatenate([vectors, jnp.broadcast_to(energies[None], (vecs, side))], axis=0)
    first = exchange(jnp.broadcast_to(first[None], (cols, *first.shape)), "col")
    all_codes = exchange(
        jnp.broadcast_to(safe_code[None, None], (reps, 1, slots)), REP
    ).reshape(reps, slots)
    order = rep_index ^ jnp.arange(reps, dtype=jnp.int32)
    codes = all_codes[order].reshape(reps * slots)
    table = jnp.stack([codes // rows, codes % rows])
    me = col_index.astype(jnp.int32).reshape(1)

    row_shape = (rows, 2 * vecs, side)
    state_shape = (cols, vecs, side)
    col_shape = (cols, cols + 1, vecs, side)

    def row_step(body, *arrays):
        send, x = call(body, [row_shape, state_shape], (table, me), (*arrays, *groups), [])
        return exchange(send, ROW), x

    def col_step(got):
        (send,) = call(direct_kernel, [col_shape], (table,), (got, *groups), [state_shape])
        return exchange(send, "col")

    got, _ = row_step(start_kernel, first)
    got = col_step(got)
    got, x1 = row_step(second_kernel, first, got)
    got = col_step(got)
    got, x2 = row_step(third_kernel, first, x1, got)
    send, part = call(
        last_direct_kernel,
        [(cols, 3, vecs, side), (vecs, side)],
        (table, me),
        (first, x2, got, *groups),
        [state_shape],
    )
    got = exchange(send, "col")
    image, send = call(
        image_kernel, [(vecs, side), (rows, 2, vecs, side)], (), (part, got), []
    )
    got = exchange(send, ROW)
    out, ritz = call(
        correct_kernel, [(vecs, side), (vecs, side)], (me,), (first, x2, image, got), []
    )
    return out, ritz[:, 0]


def solution(mesh):
    split = Mesh(
        mesh.devices.reshape(6, 4, mesh.shape["col"], 2, 2),
        ("z_lo", "x", "col", "z_hi", "core"),
    )
    return jax.shard_map(
        on_device,
        mesh=split,
        in_specs=(P(REP, ROW_COL), P(ROW_COL), P(ROW_COL_REP, None, None), P(ROW_COL_REP)),
        out_specs=(P(REP, ROW_COL), P(REP)),
        check_vma=False,
    )
```

```python
import jax
import jax.numpy as jnp
from jax import lax
from jax.experimental import pallas as pl
from jax.experimental.pallas import tpu as pltpu
from jax.sharding import Mesh
from jax.sharding import PartitionSpec as P

ROW = ("z_lo", "x")
REP = ("z_hi", "core")
ROW_COL = ("z_lo", "x", "col")
ROW_COL_REP = ("z_lo", "x", "col", "z_hi", "core")

filter_low = 5.0
filter_top = 20.0
spectrum_low = -3.0

half = (filter_top - filter_low) / 2.0
centre = (filter_top + filter_low) / 2.0
sigma_first = half / (spectrum_low - centre)
tau_value = 2.0 / sigma_first
sigma_next = 1.0 / (tau_value - sigma_first)

VMEM = pl.BlockSpec(memory_space=pltpu.VMEM)
SMEM = pl.BlockSpec(memory_space=pltpu.SMEM)


def exchange(blocks, axis):
    return lax.all_to_all(blocks, axis, 0, 0, tiled=True)


def call(body, out_shapes, scalars, arrays, scratch):
    outs = [jax.ShapeDtypeStruct(shape, jnp.float32) for shape in out_shapes]
    return pl.pallas_call(
        body,
        out_shape=outs,
        in_specs=[SMEM] * len(scalars) + [VMEM] * len(arrays),
        out_specs=[VMEM] * len(outs),
        scratch_shapes=[pltpu.VMEM(shape, jnp.float32) for shape in scratch],
    )(*scalars, *arrays)


def place(code, rows):
    shift = 16
    a = (code * (-(-(1 << shift) // rows))) >> shift
    return a, code - a * rows


def mirror_products(table, x_ref, tile_refs, send_ref, me):
    rows, vecs = send_ref.shape[0], x_ref.shape[1]
    slots = tile_refs[0].shape[0] - 1
    own = x_ref[me]
    for k in range(rows):
        send_ref[k, :vecs, :] = jnp.zeros_like(own)
        send_ref[k, vecs:, :] = own
    for group, tiles in enumerate(tile_refs):
        for slot in range(slots):
            a, k = place(table[group * slots + slot], rows)
            part = lax.dot_general(
                x_ref[a].astype(jnp.bfloat16),
                tiles[slot],
                (((1,), (0,)), ((), ())),
                preferred_element_type=jnp.float32,
            )
            send_ref[k, :vecs, :] += part


def direct_products(table, got_ref, tile_refs, sums_ref):
    vecs = sums_ref.shape[1]
    rows = got_ref.shape[0]
    slots = tile_refs[0].shape[0] - 1
    sums_ref[...] = jnp.zeros_like(sums_ref)
    for group, tiles in enumerate(tile_refs):
        for slot in range(slots):
            a, k = place(table[group * slots + slot], rows)
            part = lax.dot_general(
                got_ref[k, vecs:, :].astype(jnp.bfloat16),
                tiles[slot],
                (((1,), (1,)), ((), ())),
                preferred_element_type=jnp.float32,
            )
            sums_ref[a] += part


def summed_mirror(got_ref, vecs):
    total = got_ref[0, :vecs, :]
    for k in range(1, got_ref.shape[0]):
        total = total + got_ref[k, :vecs, :]
    return total


def start_kernel(table, me, first_ref, t0, t1, send_ref, base_ref, x_ref):
    cols, vecs = base_ref.shape[0], base_ref.shape[1] // 2
    halves = first_ref.shape[0] // cols
    for a in range(cols):
        for z in range(halves):
            x_ref[a, z * vecs : (z + 1) * vecs, :] = first_ref[a * halves + z, :vecs, :]
        base_ref[a] = first_ref[a * halves + me[1]]
    mirror_products(table, x_ref, (t0, t1), send_ref, me[0])


def product_rows(got_ref, a):
    peers, cols = got_ref.shape[0], got_ref.shape[1] - 1
    halves = peers // cols
    total = got_ref[a * halves, cols]
    for z in range(1, halves):
        total = total + got_ref[a * halves + z, cols]
    for c in range(peers):
        total = total + got_ref[c, a]
    return total


def second_kernel(table, me, first_ref, got_ref, t0, t1, t2, t3, send_ref, x_ref):
    cols = first_ref.shape[0]
    vecs = x_ref.shape[1]
    for a in range(cols):
        x = first_ref[a, :vecs, :]
        energy = first_ref[a, vecs:, :]
        image = energy * x + product_rows(got_ref, a)
        x_ref[a] = (image - centre * x) * (sigma_first / half)
    mirror_products(table, x_ref, (t0, t1, t2, t3), send_ref, me[0])


def third_kernel(table, me, first_ref, last_ref, got_ref, t0, t1, t2, t3, send_ref, x_ref):
    cols = first_ref.shape[0]
    vecs = x_ref.shape[1]
    for a in range(cols):
        x = last_ref[a]
        energy = first_ref[a, vecs:, :]
        image = energy * x + product_rows(got_ref, a)
        x_ref[a] = (image - centre * x) * (2.0 * sigma_next / half) - (
            sigma_first * sigma_next
        ) * first_ref[a, :vecs, :]
    mirror_products(table, x_ref, (t0, t1, t2, t3), send_ref, me[0])


def direct_kernel(table, got_ref, *refs):
    *tiles, send_ref, sums_ref = refs
    direct_products(table, got_ref, tiles, sums_ref)
    cols, vecs = sums_ref.shape[0], send_ref.shape[2]
    halves = send_ref.shape[0] // cols
    mirror = summed_mirror(got_ref, vecs * halves)
    for z in range(halves):
        part = slice(z * vecs, (z + 1) * vecs)
        for c in range(cols):
            for a in range(cols):
                send_ref[c * halves + z, a] = sums_ref[a, part, :]
            send_ref[c * halves + z, cols] = mirror[part]


def last_direct_kernel(table, me, first_ref, x_ref, got_ref, t0, t1, t2, t3, send_ref, image_ref, sums_ref):
    direct_products(table, got_ref, (t0, t1, t2, t3), sums_ref)
    cols, vecs = sums_ref.shape[0], sums_ref.shape[1]
    x = x_ref[me[0]]
    image = first_ref[me[0], vecs:, :] * x + summed_mirror(got_ref, vecs)
    image_ref[...] = image
    crossed = x * image
    for a in range(cols):
        crossed = crossed + x_ref[a] * sums_ref[a]
    for c in range(cols):
        send_ref[c, 0] = sums_ref[c]
        send_ref[c, 1] = crossed
        send_ref[c, 2] = x * x


def image_kernel(part_ref, got_ref, image_ref, send_ref):
    cols = got_ref.shape[0]
    totals = [got_ref[0, i] for i in range(3)]
    for c in range(1, cols):
        totals = [total + got_ref[c, i] for i, total in enumerate(totals)]
    image_ref[...] = part_ref[...] + totals[0]
    for k in range(send_ref.shape[0]):
        send_ref[k, 0] = totals[1]
        send_ref[k, 1] = totals[2]


def correct_kernel(me, first_ref, x_all_ref, image_ref, got_ref, out_ref, ritz_ref):
    crossed, squares = got_ref[0, 0], got_ref[0, 1]
    for k in range(1, got_ref.shape[0]):
        crossed = crossed + got_ref[k, 0]
        squares = squares + got_ref[k, 1]
    ritz = jnp.sum(crossed, axis=1, keepdims=True) / (
        jnp.sum(squares, axis=1, keepdims=True) + 1e-06
    )
    x = x_all_ref[me[0]]
    vecs = x.shape[0]
    resid = image_ref[...] - ritz * x
    spacing = first_ref[me[0], vecs:, :] - ritz
    out_ref[...] = x - spacing / jnp.maximum(spacing * spacing, 1.0) * resid
    ritz_ref[...] = jnp.broadcast_to(ritz, ritz_ref.shape)


def on_device(vectors, energies, tiles, tile_codes):
    rows = lax.axis_size(ROW)
    cols = lax.axis_size("col")
    halves = lax.axis_size("z_hi")
    row_index = lax.axis_index(ROW)
    col_index = lax.axis_index("col")
    half_index = lax.axis_index("z_hi")
    slots, side = tiles.shape[0], tiles.shape[1]
    vecs = vectors.shape[0]
    present = tile_codes >= 0
    safe_code = jnp.where(present, tile_codes, 0)
    on_diagonal = present & (safe_code == col_index * rows + row_index)
    upper_mask = lax.broadcasted_iota(jnp.int32, (side, side), 1) > lax.broadcasted_iota(
        jnp.int32, (side, side), 0
    )
    keep_mask = present[:, None, None] & (
        upper_mask[None] | jnp.logical_not(on_diagonal)[:, None, None]
    )
    stored = jnp.where(keep_mask, tiles, jnp.zeros((), tiles.dtype))
    label = jnp.broadcast_to(
        jnp.pad(safe_code.astype(tiles.dtype), (0, side - slots))[None, None], (1, side, side)
    )
    stored = jnp.concatenate([stored, label], axis=0)
    swap = [(0, 1), (1, 0)]
    far = lax.ppermute(stored, "z_hi", swap)
    near = lax.ppermute(stored, "core", swap)

    def codes_of(group):
        return group[slots, 0, :slots].astype(jnp.int32)

    first = jnp.concatenate([vectors, jnp.broadcast_to(energies[None], (vecs, side))], axis=0)
    first = jnp.broadcast_to(first[None], (cols * halves, *first.shape))
    first = exchange(first, ("col", "z_hi"))
    me = jnp.stack([col_index, half_index]).astype(jnp.int32)

    state_shape = (cols, vecs, side)
    col_shape = (cols, cols + 1, vecs, side)
    pair_shape = (cols * halves, cols + 1, vecs, side)

    pair = (stored, near)
    pair_codes = jnp.concatenate([safe_code, codes_of(near)])
    send, base = call(
        start_kernel,
        [(rows, 2 * halves * vecs, side), (cols, 2 * vecs, side)],
        (pair_codes, me),
        (first, *pair),
        [(cols, halves * vecs, side)],
    )
    got = exchange(send, ROW)
    (send,) = call(
        direct_kernel, [pair_shape], (pair_codes,), (got, *pair), [(cols, halves * vecs, side)]
    )
    far, _ = lax.optimization_barrier((far, send))
    got = exchange(send, ("col", "z_hi"))
    far_near = lax.ppermute(far, "core", swap)
    groups = (stored, near, far, far_near)
    codes = jnp.concatenate([pair_codes, codes_of(far), codes_of(far_near)])

    def row_step(body, *arrays):
        send, x = call(
            body, [(rows, 2 * vecs, side), state_shape], (codes, me), (*arrays, *groups), []
        )
        return exchange(send, ROW), x

    got, x1 = row_step(second_kernel, base, got)
    (send,) = call(direct_kernel, [col_shape], (codes,), (got, *groups), [state_shape])
    got = exchange(send, "col")
    got, x2 = row_step(third_kernel, base, x1, got)
    send, part = call(
        last_direct_kernel,
        [(cols, 3, vecs, side), (vecs, side)],
        (codes, me),
        (base, x2, got, *groups),
        [state_shape],
    )
    got = exchange(send, "col")
    image, send = call(
        image_kernel, [(vecs, side), (rows, 2, vecs, side)], (), (part, got), []
    )
    got = exchange(send, ROW)
    out, ritz = call(
        correct_kernel, [(vecs, side), (vecs, side)], (me,), (base, x2, image, got), []
    )
    return out, ritz[:, 0]


def solution(mesh):
    split = Mesh(
        mesh.devices.reshape(6, 4, mesh.shape["col"], 2, 2),
        ("z_lo", "x", "col", "z_hi", "core"),
    )
    return jax.shard_map(
        on_device,
        mesh=split,
        in_specs=(P(REP, ROW_COL), P(ROW_COL), P(ROW_COL_REP, None, None), P(ROW_COL_REP)),
        out_specs=(P(REP, ROW_COL), P(REP)),
        check_vma=False,
    )
```

```python
import jax
import jax.numpy as jnp
from jax import lax
from jax.experimental import pallas as pl
from jax.experimental.pallas import tpu as pltpu
from jax.sharding import Mesh
from jax.sharding import PartitionSpec as P

ROW = ("z_lo", "x")
COL = ("col", "z_hi")
REP = ("z_hi", "core")
ROW_COL = ("z_lo", "x", "col")
ROW_COL_REP = ("z_lo", "x", "col", "z_hi", "core")

filter_low = 5.0
filter_top = 20.0
spectrum_low = -3.0

half = (filter_top - filter_low) / 2.0
centre = (filter_top + filter_low) / 2.0
sigma_first = half / (spectrum_low - centre)
tau_value = 2.0 / sigma_first
sigma_next = 1.0 / (tau_value - sigma_first)

VMEM = pl.BlockSpec(memory_space=pltpu.VMEM)
SMEM = pl.BlockSpec(memory_space=pltpu.SMEM)


def exchange(blocks, axis):
    return lax.all_to_all(blocks, axis, 0, 0, tiled=True)


def call(body, out_shapes, scalars, arrays, scratch=()):
    arrays = [pltpu.with_memory_space_constraint(a, pltpu.VMEM) for a in arrays]
    return pl.pallas_call(
        body,
        out_shape=[pltpu.VMEM(shape, jnp.float32) for shape in out_shapes],
        in_specs=[SMEM] * len(scalars) + [VMEM] * len(arrays),
        out_specs=[VMEM] * len(out_shapes),
        scratch_shapes=[pltpu.VMEM(shape, jnp.float32) for shape in scratch],
    )(*scalars, *arrays)


def place(code, rows):
    shift = 16
    a = (code * (-(-(1 << shift) // rows))) >> shift
    return a, code - a * rows


def mirror_products(codes, me, x_ref, tile_refs, send_ref):
    rows, vecs = send_ref.shape[0], x_ref.shape[1]
    slots = tile_refs[0].shape[0]
    own = x_ref[me]
    for k in range(rows):
        send_ref[k, :vecs, :] = jnp.zeros_like(own)
        send_ref[k, vecs:, :] = own
    for group, tiles in enumerate(tile_refs):
        for slot in range(slots):
            a, k = place(codes[group * slots + slot], rows)
            part = lax.dot_general(
                x_ref[a].astype(jnp.bfloat16),
                tiles[slot],
                (((1,), (0,)), ((), ())),
                preferred_element_type=jnp.float32,
            )
            send_ref[k, :vecs, :] += part


def direct_products(codes, me, got_ref, tile_refs, sums_ref):
    vecs = sums_ref.shape[1]
    rows = got_ref.shape[0]
    slots = tile_refs[0].shape[0]
    mirror = got_ref[0, :vecs, :]
    for k in range(1, rows):
        mirror = mirror + got_ref[k, :vecs, :]
    sums_ref[...] = jnp.zeros_like(sums_ref)
    sums_ref[me] = mirror
    for group, tiles in enumerate(tile_refs):
        for slot in range(slots):
            a, k = place(codes[group * slots + slot], rows)
            part = lax.dot_general(
                got_ref[k, vecs:, :].astype(jnp.bfloat16),
                tiles[slot],
                (((1,), (1,)), ((), ())),
                preferred_element_type=jnp.float32,
            )
            sums_ref[a] += part


def summed(got_ref, a):
    total = got_ref[0, a]
    for peer in range(1, got_ref.shape[0]):
        total = total + got_ref[peer, a]
    return total


def start_kernel(codes, me, first_ref, t0, t1, send_ref, base_ref):
    cols = base_ref.shape[1]
    halves = first_ref.shape[0] // cols
    vecs = first_ref.shape[1] // 2
    for a in range(cols):
        for z in range(halves):
            part = slice(z * vecs, (z + 1) * vecs)
            base_ref[0, a, part, :] = first_ref[a * halves + z, :vecs, :]
            base_ref[1, a, part, :] = first_ref[a * halves + z, vecs:, :]
    mirror_products(codes, me[0], base_ref.at[0], (t0, t1), send_ref)


def second_kernel(codes, me, base_ref, got_ref, t0, t1, send_ref, x_ref):
    for a in range(x_ref.shape[0]):
        x = base_ref[0, a]
        image = base_ref[1, a] * x + summed(got_ref, a)
        x_ref[a] = (image - centre * x) * (sigma_first / half)
    mirror_products(codes, me[0], x_ref, (t0, t1), send_ref)


def third_kernel(codes, me, base_ref, last_ref, got_ref, t0, t1, send_ref, x_ref):
    for a in range(x_ref.shape[0]):
        x = last_ref[a]
        image = base_ref[1, a] * x + summed(got_ref, a)
        x_ref[a] = (image - centre * x) * (2.0 * sigma_next / half) - (
            sigma_first * sigma_next
        ) * base_ref[0, a]
    mirror_products(codes, me[0], x_ref, (t0, t1), send_ref)


def direct_kernel(codes, me, got_ref, t0, t1, send_ref, sums_ref):
    direct_products(codes, me[0], got_ref, (t0, t1), sums_ref)
    for peer in range(send_ref.shape[0]):
        send_ref[peer] = sums_ref[...]


def last_direct_kernel(codes, me, base_ref, x_ref, got_ref, t0, t1, send_ref, sums_ref):
    direct_products(codes, me[0], got_ref, (t0, t1), sums_ref)
    cols, vecs = sums_ref.shape[0], send_ref.shape[1] // 3
    halves = send_ref.shape[0] // cols
    x = x_ref[me[0]]
    energy = base_ref[1, me[0]]
    crossed = x_ref[0] * sums_ref[0]
    for a in range(1, cols):
        crossed = crossed + x_ref[a] * sums_ref[a]
    for z in range(halves):
        part = slice(z * vecs, (z + 1) * vecs)
        once = jnp.where(me[1] == z, 1.0, 0.0)
        square = x[part] * x[part] * once
        local = crossed[part] + energy[part] * square
        for c in range(cols):
            send_ref[c * halves + z, :vecs, :] = sums_ref[c, part, :]
            send_ref[c * halves + z, vecs : 2 * vecs, :] = local
            send_ref[c * halves + z, 2 * vecs :, :] = square


def own_part(ref, index, half_index, vecs):
    block = ref[index]
    part = block[:vecs]
    for z in range(1, block.shape[0] // vecs):
        part = jnp.where(half_index == z, block[z * vecs : (z + 1) * vecs], part)
    return part


def image_kernel(got_ref, image_ref, send_ref):
    vecs = image_ref.shape[0]
    total = got_ref[0]
    for peer in range(1, got_ref.shape[0]):
        total = total + got_ref[peer]
    image_ref[...] = total[:vecs]
    for k in range(send_ref.shape[0]):
        send_ref[k] = total[vecs:]


def correct_kernel(me, base_ref, x_ref, image_ref, got_ref, out_ref, ritz_ref):
    vecs = out_ref.shape[0]
    total = got_ref[0]
    for k in range(1, got_ref.shape[0]):
        total = total + got_ref[k]
    total = jnp.sum(total, axis=1, keepdims=True)
    ritz = total[:vecs] / (total[vecs:] + 1e-06)
    x = own_part(x_ref, me[0], me[1], vecs)
    energy = base_ref[1, me[0]][:vecs]
    resid = energy * x + image_ref[...] - ritz * x
    spacing = energy - ritz
    out_ref[...] = x - spacing / jnp.maximum(spacing * spacing, 1.0) * resid
    ritz_ref[...] = jnp.broadcast_to(ritz, ritz_ref.shape)


def on_device(vectors, energies, tiles, tile_codes):
    rows = lax.axis_size(ROW)
    cols = lax.axis_size("col")
    halves = lax.axis_size("z_hi")
    row_index = lax.axis_index(ROW)
    col_index = lax.axis_index("col")
    half_index = lax.axis_index("z_hi")
    slots, side = tiles.shape[0], tiles.shape[1]
    vecs = vectors.shape[0]
    wide = vecs * halves
    present = tile_codes >= 0
    safe_code = jnp.where(present, tile_codes, 0)
    on_diagonal = present & (safe_code == col_index * rows + row_index)
    upper_mask = lax.broadcasted_iota(jnp.int32, (side, side), 1) > lax.broadcasted_iota(
        jnp.int32, (side, side), 0
    )
    keep_mask = present[:, None, None] & (
        upper_mask[None] | jnp.logical_not(on_diagonal)[:, None, None]
    )
    stored = jnp.where(keep_mask, tiles, jnp.zeros((), tiles.dtype))
    swap = [(0, 1), (1, 0)]
    near = lax.ppermute(stored, "core", swap)
    near_code = lax.ppermute(safe_code, "core", swap)
    codes = jnp.concatenate([safe_code, near_code])
    pair = (stored, near)

    first = jnp.concatenate([vectors, jnp.broadcast_to(energies[None], (vecs, side))], axis=0)
    first = exchange(jnp.broadcast_to(first[None], (cols * halves, *first.shape)), COL)
    me = jnp.stack([col_index, half_index]).astype(jnp.int32)

    row_shape = (rows, 2 * wide, side)
    state_shape = (cols, wide, side)
    col_shape = (cols * halves, cols, wide, side)
    scalars = (codes, me)

    def col_step(got):
        (send,) = call(direct_kernel, [col_shape], scalars, (got, *pair), [state_shape])
        return exchange(send, COL)

    send, base = call(start_kernel, [row_shape, (2, *state_shape)], scalars, (first, *pair))
    got = col_step(exchange(send, ROW))
    send, x1 = call(second_kernel, [row_shape, state_shape], scalars, (base, got, *pair))
    got = col_step(exchange(send, ROW))
    send, x2 = call(third_kernel, [row_shape, state_shape], scalars, (base, x1, got, *pair))
    got = exchange(send, ROW)
    (send,) = call(
        last_direct_kernel,
        [(cols * halves, 3 * vecs, side)],
        scalars,
        (base, x2, got, *pair),
        [state_shape],
    )
    got = exchange(send, COL)
    image, send = call(image_kernel, [(vecs, side), (rows, 2 * vecs, side)], (), (got,))
    got = exchange(send, ROW)
    out, ritz = call(
        correct_kernel, [(vecs, side), (vecs, side)], (me,), (base, x2, image, got)
    )
    return out, ritz[:, 0]


def solution(mesh):
    split = Mesh(
        mesh.devices.reshape(6, 4, mesh.shape["col"], 2, 2),
        ("z_lo", "x", "col", "z_hi", "core"),
    )
    return jax.shard_map(
        on_device,
        mesh=split,
        in_specs=(P(REP, ROW_COL), P(ROW_COL), P(ROW_COL_REP, None, None), P(ROW_COL_REP)),
        out_specs=(P(REP, ROW_COL), P(REP)),
        check_vma=False,
    )
```

```python
import jax
import jax.numpy as jnp
from jax import lax
from jax.experimental import pallas as pl
from jax.experimental.pallas import tpu as pltpu
from jax.sharding import Mesh
from jax.sharding import PartitionSpec as P

ROW = ("z_lo", "x")
COL = ("col", "z_hi")
REP = ("z_hi", "core")
ROW_COL = ("z_lo", "x", "col")
ROW_COL_REP = ("z_lo", "x", "col", "z_hi", "core")

filter_low = 5.0
filter_top = 20.0
spectrum_low = -3.0

half = (filter_top - filter_low) / 2.0
centre = (filter_top + filter_low) / 2.0
sigma_first = half / (spectrum_low - centre)
tau_value = 2.0 / sigma_first
sigma_next = 1.0 / (tau_value - sigma_first)

VMEM = pl.BlockSpec(memory_space=pltpu.VMEM)
SMEM = pl.BlockSpec(memory_space=pltpu.SMEM)


def exchange(blocks, axis):
    return lax.all_to_all(blocks, axis, 0, 0, tiled=True)


def call(body, out_shapes, scalars, arrays, scratch=(), space=pltpu.VMEM, hold=True):
    if hold:
        arrays = [pltpu.with_memory_space_constraint(a, pltpu.VMEM) for a in arrays]
    return pl.pallas_call(
        body,
        out_shape=[space(shape, jnp.float32) for shape in out_shapes],
        in_specs=[SMEM] * len(scalars) + [VMEM] * len(arrays),
        out_specs=[VMEM] * len(out_shapes),
        scratch_shapes=[pltpu.VMEM(shape, jnp.float32) for shape in scratch],
    )(*scalars, *arrays)


def place(code, rows):
    shift = 16
    a = (code * (-(-(1 << shift) // rows))) >> shift
    return a, code - a * rows


def mirror_products(codes, me, x_ref, tile_refs, send_ref):
    rows, vecs = send_ref.shape[0], x_ref.shape[1]
    slots = tile_refs[0].shape[0]
    own = x_ref[me]
    for k in range(rows):
        send_ref[k, :vecs, :] = jnp.zeros_like(own)
        send_ref[k, vecs:, :] = own
    for group, tiles in enumerate(tile_refs):
        for slot in range(slots):
            a, k = place(codes[group * slots + slot], rows)
            part = lax.dot_general(
                x_ref[a].astype(jnp.bfloat16),
                tiles[slot],
                (((1,), (0,)), ((), ())),
                preferred_element_type=jnp.float32,
            )
            send_ref[k, :vecs, :] += part


def direct_products(codes, me, got_ref, tile_refs, sums_ref):
    vecs = sums_ref.shape[1]
    rows = got_ref.shape[0]
    slots = tile_refs[0].shape[0]
    mirror = got_ref[0, :vecs, :]
    for k in range(1, rows):
        mirror = mirror + got_ref[k, :vecs, :]
    sums_ref[...] = jnp.zeros_like(sums_ref)
    sums_ref[me] = mirror
    for group, tiles in enumerate(tile_refs):
        for slot in range(slots):
            a, k = place(codes[group * slots + slot], rows)
            part = lax.dot_general(
                got_ref[k, vecs:, :].astype(jnp.bfloat16),
                tiles[slot],
                (((1,), (1,)), ((), ())),
                preferred_element_type=jnp.float32,
            )
            sums_ref[a] += part


def summed(got_ref, a):
    total = got_ref[0, a]
    for peer in range(1, got_ref.shape[0]):
        total = total + got_ref[peer, a]
    return total


def spread_kernel(vectors_ref, energies_ref, send_ref):
    vecs = vectors_ref.shape[0]
    energy = jnp.broadcast_to(energies_ref[...], vectors_ref.shape)
    for peer in range(send_ref.shape[0]):
        send_ref[peer, :vecs, :] = vectors_ref[...]
        send_ref[peer, vecs:, :] = energy


def start_kernel(codes, me, first_ref, t0, t1, send_ref, base_ref):
    cols = base_ref.shape[1]
    halves = first_ref.shape[0] // cols
    vecs = first_ref.shape[1] // 2
    for a in range(cols):
        for z in range(halves):
            part = slice(z * vecs, (z + 1) * vecs)
            base_ref[0, a, part, :] = first_ref[a * halves + z, :vecs, :]
            base_ref[1, a, part, :] = first_ref[a * halves + z, vecs:, :]
    mirror_products(codes, me[0], base_ref.at[0], (t0, t1), send_ref)


def second_kernel(codes, me, base_ref, got_ref, t0, t1, send_ref, x_ref):
    for a in range(x_ref.shape[0]):
        x = base_ref[0, a]
        image = base_ref[1, a] * x + summed(got_ref, a)
        x_ref[a] = (image - centre * x) * (sigma_first / half)
    mirror_products(codes, me[0], x_ref, (t0, t1), send_ref)


def third_kernel(codes, me, base_ref, last_ref, got_ref, t0, t1, send_ref, x_ref):
    for a in range(x_ref.shape[0]):
        x = last_ref[a]
        image = base_ref[1, a] * x + summed(got_ref, a)
        x_ref[a] = (image - centre * x) * (2.0 * sigma_next / half) - (
            sigma_first * sigma_next
        ) * base_ref[0, a]
    mirror_products(codes, me[0], x_ref, (t0, t1), send_ref)


def direct_kernel(codes, me, got_ref, t0, t1, send_ref, sums_ref):
    direct_products(codes, me[0], got_ref, (t0, t1), sums_ref)
    for peer in range(send_ref.shape[0]):
        send_ref[peer] = sums_ref[...]


def last_direct_kernel(codes, me, base_ref, x_ref, got_ref, t0, t1, send_ref, sums_ref):
    direct_products(codes, me[0], got_ref, (t0, t1), sums_ref)
    cols, vecs = sums_ref.shape[0], send_ref.shape[1] // 3
    halves = send_ref.shape[0] // cols
    x = x_ref[me[0]]
    energy = base_ref[1, me[0]]
    crossed = x_ref[0] * sums_ref[0]
    for a in range(1, cols):
        crossed = crossed + x_ref[a] * sums_ref[a]
    for z in range(halves):
        part = slice(z * vecs, (z + 1) * vecs)
        once = jnp.where(me[1] == z, 1.0, 0.0)
        square = x[part] * x[part] * once
        local = crossed[part] + energy[part] * square
        for c in range(cols):
            send_ref[c * halves + z, :vecs, :] = sums_ref[c, part, :]
            send_ref[c * halves + z, vecs : 2 * vecs, :] = local
            send_ref[c * halves + z, 2 * vecs :, :] = square


def own_part(ref, index, half_index, vecs):
    block = ref[index]
    part = block[:vecs]
    for z in range(1, block.shape[0] // vecs):
        part = jnp.where(half_index == z, block[z * vecs : (z + 1) * vecs], part)
    return part


def image_kernel(got_ref, image_ref, send_ref):
    vecs = image_ref.shape[0]
    total = got_ref[0]
    for peer in range(1, got_ref.shape[0]):
        total = total + got_ref[peer]
    image_ref[...] = total[:vecs]
    for k in range(send_ref.shape[0]):
        send_ref[k] = total[vecs:]


def correct_kernel(me, base_ref, x_ref, image_ref, got_ref, out_ref, ritz_ref):
    vecs = out_ref.shape[0]
    total = got_ref[0]
    for k in range(1, got_ref.shape[0]):
        total = total + got_ref[k]
    total = jnp.sum(total, axis=1, keepdims=True)
    ritz = total[:vecs] / (total[vecs:] + 1e-06)
    x = own_part(x_ref, me[0], me[1], vecs)
    energy = base_ref[1, me[0]][:vecs]
    resid = energy * x + image_ref[...] - ritz * x
    spacing = energy - ritz
    out_ref[...] = x - spacing / jnp.maximum(spacing * spacing, 1.0) * resid
    row = jnp.broadcast_to(ritz[:1], (1, x.shape[1]))
    lane = lax.broadcasted_iota(jnp.int32, row.shape, 1)
    for v in range(1, vecs):
        row = jnp.where(lane == v, ritz[v : v + 1], row)
    ritz_ref[...] = row[:, :vecs]


def on_device(vectors, energies, tiles, tile_codes):
    rows = lax.axis_size(ROW)
    cols = lax.axis_size("col")
    halves = lax.axis_size("z_hi")
    row_index = lax.axis_index(ROW)
    col_index = lax.axis_index("col")
    half_index = lax.axis_index("z_hi")
    side = tiles.shape[1]
    vecs = vectors.shape[0]
    wide = vecs * halves
    present = tile_codes >= 0
    safe_code = jnp.where(present, tile_codes, 0)
    on_diagonal = present & (safe_code == col_index * rows + row_index)
    upper_mask = lax.broadcasted_iota(jnp.int32, (side, side), 1) > lax.broadcasted_iota(
        jnp.int32, (side, side), 0
    )
    keep_mask = present[:, None, None] & (
        upper_mask[None] | jnp.logical_not(on_diagonal)[:, None, None]
    )
    stored = jnp.where(keep_mask, tiles, jnp.zeros((), tiles.dtype))
    swap = [(0, 1), (1, 0)]
    near = lax.ppermute(stored, "core", swap)
    near_code = lax.ppermute(safe_code, "core", swap)
    codes = jnp.concatenate([safe_code, near_code])
    pair = (stored, near)

    (first,) = call(
        spread_kernel,
        [(cols * halves, 2 * vecs, side)],
        (),
        (vectors, energies[None]),
        hold=False,
    )
    first = exchange(first, COL)
    me = jnp.stack([col_index, half_index]).astype(jnp.int32)

    row_shape = (rows, 2 * wide, side)
    state_shape = (cols, wide, side)
    col_shape = (cols * halves, cols, wide, side)
    scalars = (codes, me)

    def col_step(got):
        (send,) = call(direct_kernel, [col_shape], scalars, (got, *pair), [state_shape])
        return exchange(send, COL)

    send, base = call(start_kernel, [row_shape, (2, *state_shape)], scalars, (first, *pair))
    got = col_step(exchange(send, ROW))
    send, x1 = call(second_kernel, [row_shape, state_shape], scalars, (base, got, *pair))
    got = col_step(exchange(send, ROW))
    send, x2 = call(third_kernel, [row_shape, state_shape], scalars, (base, x1, got, *pair))
    got = exchange(send, ROW)
    (send,) = call(
        last_direct_kernel,
        [(cols * halves, 3 * vecs, side)],
        scalars,
        (base, x2, got, *pair),
        [state_shape],
    )
    got = exchange(send, COL)
    image, send = call(image_kernel, [(vecs, side), (rows, 2 * vecs, side)], (), (got,))
    got = exchange(send, ROW)
    out, ritz = call(
        correct_kernel,
        [(vecs, side), (1, vecs)],
        (me,),
        (base, x2, image, got),
        space=jax.ShapeDtypeStruct,
    )
    return out, ritz[0]


def solution(mesh):
    split = Mesh(
        mesh.devices.reshape(6, 4, mesh.shape["col"], 2, 2),
        ("z_lo", "x", "col", "z_hi", "core"),
    )
    return jax.shard_map(
        on_device,
        mesh=split,
        in_specs=(P(REP, ROW_COL), P(ROW_COL), P(ROW_COL_REP, None, None), P(ROW_COL_REP)),
        out_specs=(P(REP, ROW_COL), P(REP)),
        check_vma=False,
    )
```

```python
import jax
import jax.numpy as jnp
from jax import lax
from jax.experimental import pallas as pl
from jax.experimental.pallas import tpu as pltpu
from jax.sharding import Mesh
from jax.sharding import PartitionSpec as P

ROW = ("z_lo", "x")
COL = ("col", "z_hi")
REP = ("z_hi", "core")
ROW_COL = ("z_lo", "x", "col")
ROW_COL_REP = ("z_lo", "x", "col", "z_hi", "core")

filter_low = 5.0
filter_top = 20.0
spectrum_low = -3.0

half = (filter_top - filter_low) / 2.0
centre = (filter_top + filter_low) / 2.0
sigma_first = half / (spectrum_low - centre)
tau_value = 2.0 / sigma_first
sigma_next = 1.0 / (tau_value - sigma_first)

VMEM = pl.BlockSpec(memory_space=pltpu.VMEM)
SMEM = pl.BlockSpec(memory_space=pltpu.SMEM)


def exchange(blocks, axis):
    return lax.all_to_all(blocks, axis, 0, 0, tiled=True)


def call(body, out_shapes, scalars, arrays, scratch=(), space=pltpu.VMEM):
    arrays = [pltpu.with_memory_space_constraint(a, pltpu.VMEM) for a in arrays]
    return pl.pallas_call(
        body,
        out_shape=[space(shape, jnp.float32) for shape in out_shapes],
        in_specs=[SMEM] * len(scalars) + [VMEM] * len(arrays),
        out_specs=[VMEM] * len(out_shapes),
        scratch_shapes=[pltpu.VMEM(shape, jnp.float32) for shape in scratch],
    )(*scalars, *arrays)


def place(code, rows):
    shift = 16
    a = (code * (-(-(1 << shift) // rows))) >> shift
    return a, code - a * rows


def mirror_products(codes, me, x_ref, tile_refs, send_ref):
    rows, vecs = send_ref.shape[0], x_ref.shape[1]
    slots = tile_refs[0].shape[0] - 1
    own = x_ref[me]
    for k in range(rows):
        send_ref[k, :vecs, :] = jnp.zeros_like(own)
        send_ref[k, vecs:, :] = own
    for group, tiles in enumerate(tile_refs):
        for slot in range(slots):
            a, k = place(codes[group * slots + slot], rows)
            part = lax.dot_general(
                x_ref[a].astype(jnp.bfloat16),
                tiles[slot],
                (((1,), (0,)), ((), ())),
                preferred_element_type=jnp.float32,
            )
            send_ref[k, :vecs, :] += part


def direct_products(codes, me, got_ref, tile_refs, sums_ref):
    vecs = sums_ref.shape[1]
    rows = got_ref.shape[0]
    slots = tile_refs[0].shape[0] - 1
    mirror = got_ref[0, :vecs, :]
    for k in range(1, rows):
        mirror = mirror + got_ref[k, :vecs, :]
    sums_ref[...] = jnp.zeros_like(sums_ref)
    sums_ref[me] = mirror
    for group, tiles in enumerate(tile_refs):
        for slot in range(slots):
            a, k = place(codes[group * slots + slot], rows)
            part = lax.dot_general(
                got_ref[k, vecs:, :].astype(jnp.bfloat16),
                tiles[slot],
                (((1,), (1,)), ((), ())),
                preferred_element_type=jnp.float32,
            )
            sums_ref[a] += part


def summed(got_ref, a):
    total = got_ref[0, a]
    for peer in range(1, got_ref.shape[0]):
        total = total + got_ref[peer, a]
    return total


def prepare_kernel(codes, me, vectors_ref, energies_ref, tiles_ref, send_ref, stored_ref):
    vecs = vectors_ref.shape[0]
    slots, side = tiles_ref.shape[0], tiles_ref.shape[1]
    energy = jnp.broadcast_to(energies_ref[...], vectors_ref.shape)
    for peer in range(send_ref.shape[0]):
        send_ref[peer, :vecs, :] = vectors_ref[...]
        send_ref[peer, vecs:, :] = energy
    line = lax.broadcasted_iota(jnp.int32, (side, side), 0)
    lane = lax.broadcasted_iota(jnp.int32, (side, side), 1)
    label = jnp.zeros((side, side), jnp.float32)
    for slot in range(slots):
        code = codes[slot]
        bound = jnp.where(code < 0, -side, jnp.where(code == me[2], 0, side))
        tile = tiles_ref[slot].astype(jnp.float32)
        stored_ref[slot] = jnp.where(line - lane < bound, tile, 0.0).astype(stored_ref.dtype)
        label = jnp.where(lane == slot, jnp.maximum(code, 0).astype(jnp.float32), label)
    stored_ref[slots] = label.astype(stored_ref.dtype)


def start_kernel(me, first_ref, t0, t1, send_ref, base_ref, codes):
    cols = base_ref.shape[1]
    halves = first_ref.shape[0] // cols
    vecs = first_ref.shape[1] // 2
    slots = t0.shape[0] - 1
    for group, tiles in enumerate((t0, t1)):
        row = tiles[slots, :1, :].astype(jnp.float32)
        for slot in range(slots):
            codes[group * slots + slot] = row[0, slot].astype(jnp.int32)
    for a in range(cols):
        for z in range(halves):
            part = slice(z * vecs, (z + 1) * vecs)
            base_ref[0, a, part, :] = first_ref[a * halves + z, :vecs, :]
            base_ref[1, a, part, :] = first_ref[a * halves + z, vecs:, :]
    mirror_products(codes, me[0], base_ref.at[0], (t0, t1), send_ref)


def second_kernel(codes, me, base_ref, got_ref, t0, t1, send_ref, x_ref):
    for a in range(x_ref.shape[0]):
        x = base_ref[0, a]
        image = base_ref[1, a] * x + summed(got_ref, a)
        x_ref[a] = (image - centre * x) * (sigma_first / half)
    mirror_products(codes, me[0], x_ref, (t0, t1), send_ref)


def third_kernel(codes, me, base_ref, last_ref, got_ref, t0, t1, send_ref, x_ref):
    for a in range(x_ref.shape[0]):
        x = last_ref[a]
        image = base_ref[1, a] * x + summed(got_ref, a)
        x_ref[a] = (image - centre * x) * (2.0 * sigma_next / half) - (
            sigma_first * sigma_next
        ) * base_ref[0, a]
    mirror_products(codes, me[0], x_ref, (t0, t1), send_ref)


def direct_kernel(codes, me, got_ref, t0, t1, send_ref, sums_ref):
    direct_products(codes, me[0], got_ref, (t0, t1), sums_ref)
    for peer in range(send_ref.shape[0]):
        send_ref[peer] = sums_ref[...]


def last_direct_kernel(codes, me, base_ref, x_ref, got_ref, t0, t1, send_ref, sums_ref):
    direct_products(codes, me[0], got_ref, (t0, t1), sums_ref)
    cols, vecs = sums_ref.shape[0], send_ref.shape[1] // 3
    halves = send_ref.shape[0] // cols
    x = x_ref[me[0]]
    energy = base_ref[1, me[0]]
    crossed = x_ref[0] * sums_ref[0]
    for a in range(1, cols):
        crossed = crossed + x_ref[a] * sums_ref[a]
    for z in range(halves):
        part = slice(z * vecs, (z + 1) * vecs)
        once = jnp.where(me[1] == z, 1.0, 0.0)
        square = x[part] * x[part] * once
        local = crossed[part] + energy[part] * square
        for c in range(cols):
            send_ref[c * halves + z, :vecs, :] = sums_ref[c, part, :]
            send_ref[c * halves + z, vecs : 2 * vecs, :] = local
            send_ref[c * halves + z, 2 * vecs :, :] = square


def own_part(ref, index, half_index, vecs):
    block = ref[index]
    part = block[:vecs]
    for z in range(1, block.shape[0] // vecs):
        part = jnp.where(half_index == z, block[z * vecs : (z + 1) * vecs], part)
    return part


def image_kernel(got_ref, image_ref, send_ref):
    vecs = image_ref.shape[0]
    total = got_ref[0]
    for peer in range(1, got_ref.shape[0]):
        total = total + got_ref[peer]
    image_ref[...] = total[:vecs]
    for k in range(send_ref.shape[0]):
        send_ref[k] = total[vecs:]


def correct_kernel(me, base_ref, x_ref, image_ref, got_ref, out_ref, ritz_ref):
    vecs = out_ref.shape[0]
    total = got_ref[0]
    for k in range(1, got_ref.shape[0]):
        total = total + got_ref[k]
    total = jnp.sum(total, axis=1, keepdims=True)
    ritz = total[:vecs] / (total[vecs:] + 1e-06)
    x = own_part(x_ref, me[0], me[1], vecs)
    energy = base_ref[1, me[0]][:vecs]
    resid = energy * x + image_ref[...] - ritz * x
    spacing = energy - ritz
    out_ref[...] = x - spacing / jnp.maximum(spacing * spacing, 1.0) * resid
    row = jnp.broadcast_to(ritz[:1], (1, x.shape[1]))
    lane = lax.broadcasted_iota(jnp.int32, row.shape, 1)
    for v in range(1, vecs):
        row = jnp.where(lane == v, ritz[v : v + 1], row)
    ritz_ref[...] = row[:, :vecs]


def on_device(vectors, energies, tiles, tile_codes):
    rows = lax.axis_size(ROW)
    cols = lax.axis_size("col")
    halves = lax.axis_size("z_hi")
    row_index = lax.axis_index(ROW)
    col_index = lax.axis_index("col")
    half_index = lax.axis_index("z_hi")
    slots, side = tiles.shape[0], tiles.shape[1]
    vecs = vectors.shape[0]
    wide = vecs * halves
    me = jnp.stack([col_index, half_index, col_index * rows + row_index]).astype(jnp.int32)
    first, stored = pl.pallas_call(
        prepare_kernel,
        out_shape=[
            jax.ShapeDtypeStruct((cols * halves, 2 * vecs, side), jnp.float32),
            pltpu.VMEM((slots + 1, side, side), tiles.dtype),
        ],
        in_specs=[SMEM] * 2 + [VMEM] * 3,
        out_specs=[VMEM] * 2,
    )(tile_codes, me, vectors, energies[None], tiles)
    first = exchange(first, COL)
    near = lax.ppermute(stored, "core", [(0, 1), (1, 0)])
    pair = (stored, near)

    row_shape = (rows, 2 * wide, side)
    state_shape = (cols, wide, side)
    col_shape = (cols * halves, cols, wide, side)
    send, base, codes = pl.pallas_call(
        start_kernel,
        out_shape=[
            pltpu.VMEM(row_shape, jnp.float32),
            pltpu.VMEM((2, *state_shape), jnp.float32),
            jax.ShapeDtypeStruct((2 * slots,), jnp.int32),
        ],
        in_specs=[SMEM] + [VMEM] * 3,
        out_specs=[VMEM, VMEM, SMEM],
    )(me, *(pltpu.with_memory_space_constraint(a, pltpu.VMEM) for a in (first, *pair)))
    scalars = (codes, me)

    def col_step(got):
        (send,) = call(direct_kernel, [col_shape], scalars, (got, *pair), [state_shape])
        return exchange(send, COL)

    got = col_step(exchange(send, ROW))
    send, x1 = call(second_kernel, [row_shape, state_shape], scalars, (base, got, *pair))
    got = col_step(exchange(send, ROW))
    send, x2 = call(third_kernel, [row_shape, state_shape], scalars, (base, x1, got, *pair))
    got = exchange(send, ROW)
    (send,) = call(
        last_direct_kernel,
        [(cols * halves, 3 * vecs, side)],
        scalars,
        (base, x2, got, *pair),
        [state_shape],
    )
    got = exchange(send, COL)
    image, send = call(image_kernel, [(vecs, side), (rows, 2 * vecs, side)], (), (got,))
    got = exchange(send, ROW)
    out, ritz = call(
        correct_kernel,
        [(vecs, side), (1, vecs)],
        (me,),
        (base, x2, image, got),
        space=jax.ShapeDtypeStruct,
    )
    return out, ritz[0]


def solution(mesh):
    split = Mesh(
        mesh.devices.reshape(6, 4, mesh.shape["col"], 2, 2),
        ("z_lo", "x", "col", "z_hi", "core"),
    )
    return jax.shard_map(
        on_device,
        mesh=split,
        in_specs=(P(REP, ROW_COL), P(ROW_COL), P(ROW_COL_REP, None, None), P(ROW_COL_REP)),
        out_specs=(P(REP, ROW_COL), P(REP)),
        check_vma=False,
    )
```

```python
import jax
import jax.numpy as jnp
from jax import lax
from jax.experimental import pallas as pl
from jax.experimental.pallas import tpu as pltpu
from jax.sharding import Mesh
from jax.sharding import PartitionSpec as P

ROW = ("z_lo", "x")
COL = ("col", "z_hi")
REP = ("z_hi", "core")
ROW_COL = ("z_lo", "x", "col")
ROW_COL_REP = ("z_lo", "x", "col", "z_hi", "core")

filter_low = 5.0
filter_top = 20.0
spectrum_low = -3.0

half = (filter_top - filter_low) / 2.0
centre = (filter_top + filter_low) / 2.0
sigma_first = half / (spectrum_low - centre)
tau_value = 2.0 / sigma_first
sigma_next = 1.0 / (tau_value - sigma_first)

VMEM = pl.BlockSpec(memory_space=pltpu.VMEM)
SMEM = pl.BlockSpec(memory_space=pltpu.SMEM)


def exchange(blocks, axis):
    return lax.all_to_all(blocks, axis, 0, 0, tiled=True)


def call(body, out_shapes, scalars, arrays, scratch=(), space=pltpu.VMEM):
    arrays = [pltpu.with_memory_space_constraint(a, pltpu.VMEM) for a in arrays]
    scalars = [pltpu.with_memory_space_constraint(a, pltpu.SMEM) for a in scalars]
    return pl.pallas_call(
        body,
        out_shape=[space(shape, jnp.float32) for shape in out_shapes],
        in_specs=[SMEM] * len(scalars) + [VMEM] * len(arrays),
        out_specs=[VMEM] * len(out_shapes),
        scratch_shapes=[pltpu.VMEM(shape, jnp.float32) for shape in scratch],
    )(*scalars, *arrays)


def place(code, rows):
    shift = 16
    a = (code * (-(-(1 << shift) // rows))) >> shift
    return a, code - a * rows


def mirror_products(codes, me, x_ref, tile_refs, send_ref):
    rows, vecs = send_ref.shape[0], x_ref.shape[1]
    slots = tile_refs[0].shape[0] - 1
    own = x_ref[me]
    for k in range(rows):
        send_ref[k, :vecs, :] = jnp.zeros_like(own)
        send_ref[k, vecs:, :] = own
    for group, tiles in enumerate(tile_refs):
        for slot in range(slots):
            a, k = place(codes[group * slots + slot], rows)
            part = lax.dot_general(
                x_ref[a].astype(jnp.bfloat16),
                tiles[slot],
                (((1,), (0,)), ((), ())),
                preferred_element_type=jnp.float32,
            )
            send_ref[k, :vecs, :] += part


def direct_products(codes, me, got_ref, tile_refs, sums_ref):
    vecs = sums_ref.shape[1]
    rows = got_ref.shape[0]
    slots = tile_refs[0].shape[0] - 1
    mirror = got_ref[0, :vecs, :]
    for k in range(1, rows):
        mirror = mirror + got_ref[k, :vecs, :]
    sums_ref[...] = jnp.zeros_like(sums_ref)
    sums_ref[me] = mirror
    for group, tiles in enumerate(tile_refs):
        for slot in range(slots):
            a, k = place(codes[group * slots + slot], rows)
            part = lax.dot_general(
                got_ref[k, vecs:, :].astype(jnp.bfloat16),
                tiles[slot],
                (((1,), (1,)), ((), ())),
                preferred_element_type=jnp.float32,
            )
            sums_ref[a] += part


def summed(got_ref, a):
    total = got_ref[0, a]
    for peer in range(1, got_ref.shape[0]):
        total = total + got_ref[peer, a]
    return total


def prepare_kernel(codes, vectors_ref, energies_ref, tiles_ref, send_ref, stored_ref, me):
    vecs = vectors_ref.shape[0]
    slots, side = tiles_ref.shape[0], tiles_ref.shape[1]
    energy = jnp.broadcast_to(energies_ref[...], vectors_ref.shape)
    for peer in range(send_ref.shape[0]):
        send_ref[peer, :vecs, :] = vectors_ref[...]
        send_ref[peer, vecs:, :] = energy
    col_index = lax.axis_index("col")
    me[0] = col_index
    me[1] = lax.axis_index("z_hi")
    diagonal = col_index * lax.axis_size(ROW) + lax.axis_index(ROW)
    line = lax.broadcasted_iota(jnp.int32, (side, side), 0)
    lane = lax.broadcasted_iota(jnp.int32, (side, side), 1)
    label = jnp.zeros((side, side), jnp.float32)
    for slot in range(slots):
        code = codes[slot]
        bound = jnp.where(code < 0, -side, jnp.where(code == diagonal, 0, side))
        tile = tiles_ref[slot].astype(jnp.float32)
        stored_ref[slot] = jnp.where(line - lane < bound, tile, 0.0).astype(stored_ref.dtype)
        label = jnp.where(lane == slot, jnp.maximum(code, 0).astype(jnp.float32), label)
    stored_ref[slots] = label.astype(stored_ref.dtype)


def start_kernel(me, first_ref, t0, t1, send_ref, base_ref, codes):
    cols = base_ref.shape[1]
    halves = first_ref.shape[0] // cols
    vecs = first_ref.shape[1] // 2
    slots = t0.shape[0] - 1
    for group, tiles in enumerate((t0, t1)):
        row = tiles[slots, :1, :].astype(jnp.float32)
        for slot in range(slots):
            codes[group * slots + slot] = row[0, slot].astype(jnp.int32)
    for a in range(cols):
        for z in range(halves):
            part = slice(z * vecs, (z + 1) * vecs)
            base_ref[0, a, part, :] = first_ref[a * halves + z, :vecs, :]
            base_ref[1, a, part, :] = first_ref[a * halves + z, vecs:, :]
    mirror_products(codes, me[0], base_ref.at[0], (t0, t1), send_ref)


def second_kernel(codes, me, base_ref, got_ref, t0, t1, send_ref, x_ref):
    for a in range(x_ref.shape[0]):
        x = base_ref[0, a]
        image = base_ref[1, a] * x + summed(got_ref, a)
        x_ref[a] = (image - centre * x) * (sigma_first / half)
    mirror_products(codes, me[0], x_ref, (t0, t1), send_ref)


def third_kernel(codes, me, base_ref, last_ref, got_ref, t0, t1, send_ref, x_ref):
    for a in range(x_ref.shape[0]):
        x = last_ref[a]
        image = base_ref[1, a] * x + summed(got_ref, a)
        x_ref[a] = (image - centre * x) * (2.0 * sigma_next / half) - (
            sigma_first * sigma_next
        ) * base_ref[0, a]
    mirror_products(codes, me[0], x_ref, (t0, t1), send_ref)


def direct_kernel(codes, me, got_ref, t0, t1, send_ref, sums_ref):
    direct_products(codes, me[0], got_ref, (t0, t1), sums_ref)
    for peer in range(send_ref.shape[0]):
        send_ref[peer] = sums_ref[...]


def last_direct_kernel(codes, me, base_ref, x_ref, got_ref, t0, t1, send_ref, sums_ref):
    direct_products(codes, me[0], got_ref, (t0, t1), sums_ref)
    cols, vecs = sums_ref.shape[0], send_ref.shape[1] // 3
    halves = send_ref.shape[0] // cols
    x = x_ref[me[0]]
    energy = base_ref[1, me[0]]
    crossed = x_ref[0] * sums_ref[0]
    for a in range(1, cols):
        crossed = crossed + x_ref[a] * sums_ref[a]
    for z in range(halves):
        part = slice(z * vecs, (z + 1) * vecs)
        once = jnp.where(me[1] == z, 1.0, 0.0)
        square = x[part] * x[part] * once
        local = crossed[part] + energy[part] * square
        for c in range(cols):
            send_ref[c * halves + z, :vecs, :] = sums_ref[c, part, :]
            send_ref[c * halves + z, vecs : 2 * vecs, :] = local
            send_ref[c * halves + z, 2 * vecs :, :] = square


def own_part(ref, index, half_index, vecs):
    block = ref[index]
    part = block[:vecs]
    for z in range(1, block.shape[0] // vecs):
        part = jnp.where(half_index == z, block[z * vecs : (z + 1) * vecs], part)
    return part


def image_kernel(got_ref, image_ref, send_ref):
    vecs = image_ref.shape[0]
    total = got_ref[0]
    for peer in range(1, got_ref.shape[0]):
        total = total + got_ref[peer]
    image_ref[...] = total[:vecs]
    for k in range(send_ref.shape[0]):
        send_ref[k] = total[vecs:]


def correct_kernel(me, base_ref, x_ref, image_ref, got_ref, out_ref, ritz_ref):
    vecs = out_ref.shape[0]
    total = got_ref[0]
    for k in range(1, got_ref.shape[0]):
        total = total + got_ref[k]
    total = jnp.sum(total, axis=1, keepdims=True)
    ritz = total[:vecs] / (total[vecs:] + 1e-06)
    x = own_part(x_ref, me[0], me[1], vecs)
    energy = base_ref[1, me[0]][:vecs]
    resid = energy * x + image_ref[...] - ritz * x
    spacing = energy - ritz
    out_ref[...] = x - spacing / jnp.maximum(spacing * spacing, 1.0) * resid
    row = jnp.broadcast_to(ritz[:1], (1, x.shape[1]))
    lane = lax.broadcasted_iota(jnp.int32, row.shape, 1)
    for v in range(1, vecs):
        row = jnp.where(lane == v, ritz[v : v + 1], row)
    ritz_ref[...] = row[:, :vecs]


def on_device(vectors, energies, tiles, tile_codes):
    rows = lax.axis_size(ROW)
    cols = lax.axis_size("col")
    halves = lax.axis_size("z_hi")
    slots, side = tiles.shape[0], tiles.shape[1]
    vecs = vectors.shape[0]
    wide = vecs * halves
    first, stored, me = pl.pallas_call(
        prepare_kernel,
        out_shape=[
            jax.ShapeDtypeStruct((cols * halves, 2 * vecs, side), jnp.float32),
            pltpu.VMEM((slots + 1, side, side), tiles.dtype),
            pltpu.SMEM((2,), jnp.int32),
        ],
        in_specs=[SMEM] + [VMEM] * 3,
        out_specs=[VMEM, VMEM, SMEM],
    )(tile_codes, vectors, energies[None], tiles)
    first = exchange(first, COL)
    near = lax.ppermute(stored, "core", [(0, 1), (1, 0)])
    pair = (stored, near)

    row_shape = (rows, 2 * wide, side)
    state_shape = (cols, wide, side)
    col_shape = (cols * halves, cols, wide, side)
    send, base, codes = pl.pallas_call(
        start_kernel,
        out_shape=[
            pltpu.VMEM(row_shape, jnp.float32),
            pltpu.VMEM((2, *state_shape), jnp.float32),
            pltpu.SMEM((2 * slots,), jnp.int32),
        ],
        in_specs=[SMEM] + [VMEM] * 3,
        out_specs=[VMEM, VMEM, SMEM],
    )(
        pltpu.with_memory_space_constraint(me, pltpu.SMEM),
        *(pltpu.with_memory_space_constraint(a, pltpu.VMEM) for a in (first, *pair)),
    )
    scalars = (codes, me)

    def col_step(got):
        (send,) = call(direct_kernel, [col_shape], scalars, (got, *pair), [state_shape])
        return exchange(send, COL)

    got = col_step(exchange(send, ROW))
    send, x1 = call(second_kernel, [row_shape, state_shape], scalars, (base, got, *pair))
    got = col_step(exchange(send, ROW))
    send, x2 = call(third_kernel, [row_shape, state_shape], scalars, (base, x1, got, *pair))
    got = exchange(send, ROW)
    (send,) = call(
        last_direct_kernel,
        [(cols * halves, 3 * vecs, side)],
        scalars,
        (base, x2, got, *pair),
        [state_shape],
    )
    got = exchange(send, COL)
    image, send = call(image_kernel, [(vecs, side), (rows, 2 * vecs, side)], (), (got,))
    got = exchange(send, ROW)
    out, ritz = call(
        correct_kernel,
        [(vecs, side), (1, vecs)],
        (me,),
        (base, x2, image, got),
        space=jax.ShapeDtypeStruct,
    )
    return out, ritz[0]


def solution(mesh):
    split = Mesh(
        mesh.devices.reshape(6, 4, mesh.shape["col"], 2, 2),
        ("z_lo", "x", "col", "z_hi", "core"),
    )
    return jax.shard_map(
        on_device,
        mesh=split,
        in_specs=(P(REP, ROW_COL), P(ROW_COL), P(ROW_COL_REP, None, None), P(ROW_COL_REP)),
        out_specs=(P(REP, ROW_COL), P(REP)),
        check_vma=False,
    )
```

```python
import jax
import jax.numpy as jnp
from jax import lax
from jax.experimental import pallas as pl
from jax.experimental.pallas import tpu as pltpu
from jax.sharding import Mesh
from jax.sharding import PartitionSpec as P

ROW = ("z_lo", "x")
COL = "col"
REP = ("z_hi", "core")
ROW_COL = ("z_lo", "x", "col")
ROW_COL_REP = ("z_lo", "x", "col", "z_hi", "core")

filter_low = 5.0
filter_top = 20.0
spectrum_low = -3.0

half = (filter_top - filter_low) / 2.0
centre = (filter_top + filter_low) / 2.0
sigma_first = half / (spectrum_low - centre)
tau_value = 2.0 / sigma_first
sigma_next = 1.0 / (tau_value - sigma_first)

VMEM = pl.BlockSpec(memory_space=pltpu.VMEM)
SMEM = pl.BlockSpec(memory_space=pltpu.SMEM)


def exchange(blocks, axis):
    return lax.all_to_all(blocks, axis, 0, 0, tiled=True)


def call(body, out_shapes, scalars, arrays, scratch=(), space=pltpu.VMEM):
    arrays = [pltpu.with_memory_space_constraint(a, pltpu.VMEM) for a in arrays]
    scalars = [pltpu.with_memory_space_constraint(a, pltpu.SMEM) for a in scalars]
    return pl.pallas_call(
        body,
        out_shape=[space(shape, jnp.float32) for shape in out_shapes],
        in_specs=[SMEM] * len(scalars) + [VMEM] * len(arrays),
        out_specs=[VMEM] * len(out_shapes),
        scratch_shapes=[pltpu.VMEM(shape, jnp.float32) for shape in scratch],
    )(*scalars, *arrays)


def place(code, rows):
    shift = 16
    a = (code * (-(-(1 << shift) // rows))) >> shift
    return a, code - a * rows


def mirror_products(codes, me, x_ref, tile_refs, send_ref):
    rows, vecs = send_ref.shape[0], x_ref.shape[1]
    slots = tile_refs[0].shape[0] - 1
    own = x_ref[me]
    for k in range(rows):
        send_ref[k, :vecs, :] = jnp.zeros_like(own)
        send_ref[k, vecs:, :] = own
    for group, tiles in enumerate(tile_refs):
        for slot in range(slots):
            a, k = place(codes[group * slots + slot], rows)
            part = lax.dot_general(
                x_ref[a].astype(jnp.bfloat16),
                tiles[slot],
                (((1,), (0,)), ((), ())),
                preferred_element_type=jnp.float32,
            )
            send_ref[k, :vecs, :] += part


def direct_products(codes, me, got_ref, tile_refs, sums_ref):
    vecs = sums_ref.shape[1]
    rows = got_ref.shape[0]
    slots = tile_refs[0].shape[0] - 1
    mirror = got_ref[0, :vecs, :]
    for k in range(1, rows):
        mirror = mirror + got_ref[k, :vecs, :]
    sums_ref[...] = jnp.zeros_like(sums_ref)
    sums_ref[me] = mirror
    for group, tiles in enumerate(tile_refs):
        for slot in range(slots):
            a, k = place(codes[group * slots + slot], rows)
            part = lax.dot_general(
                got_ref[k, vecs:, :].astype(jnp.bfloat16),
                tiles[slot],
                (((1,), (1,)), ((), ())),
                preferred_element_type=jnp.float32,
            )
            sums_ref[a] += part


def summed(got_ref, a):
    total = got_ref[0, a]
    for peer in range(1, got_ref.shape[0]):
        total = total + got_ref[peer, a]
    return total


def prepare_kernel(codes, vectors_ref, energies_ref, tiles_ref, send_ref, stored_ref, me):
    vecs = vectors_ref.shape[0]
    slots, side = tiles_ref.shape[0], tiles_ref.shape[1]
    energy = jnp.broadcast_to(energies_ref[...], vectors_ref.shape)
    for peer in range(send_ref.shape[0]):
        send_ref[peer, :vecs, :] = vectors_ref[...]
        send_ref[peer, vecs:, :] = energy
    col_index = lax.axis_index("col")
    me[0] = col_index
    me[1] = lax.axis_index("z_hi")
    diagonal = col_index * lax.axis_size(ROW) + lax.axis_index(ROW)
    line = lax.broadcasted_iota(jnp.int32, (side, side), 0)
    lane = lax.broadcasted_iota(jnp.int32, (side, side), 1)
    label = jnp.zeros((side, side), jnp.float32)
    for slot in range(slots):
        code = codes[slot]
        bound = jnp.where(code < 0, -side, jnp.where(code == diagonal, 0, side))
        tile = tiles_ref[slot].astype(jnp.float32)
        stored_ref[slot] = jnp.where(line - lane < bound, tile, 0.0).astype(stored_ref.dtype)
        label = jnp.where(lane == slot, jnp.maximum(code, 0).astype(jnp.float32), label)
    stored_ref[slots] = label.astype(stored_ref.dtype)


def start_kernel(me, first_ref, t0, t1, t2, t3, send_ref, base_ref, codes):
    cols = base_ref.shape[1]
    halves = first_ref.shape[0] // cols
    vecs = first_ref.shape[1] // 2
    slots = t0.shape[0] - 1
    for group, tiles in enumerate((t0, t1, t2, t3)):
        row = tiles[slots, :1, :].astype(jnp.float32)
        for slot in range(slots):
            codes[group * slots + slot] = row[0, slot].astype(jnp.int32)
    for a in range(cols):
        for z in range(halves):
            part = slice(z * vecs, (z + 1) * vecs)
            base_ref[0, a, part, :] = first_ref[a * halves + z, :vecs, :]
            base_ref[1, a, part, :] = first_ref[a * halves + z, vecs:, :]
    mirror_products(codes, me[0], base_ref.at[0], (t0, t1, t2, t3), send_ref)


def second_kernel(codes, me, base_ref, got_ref, t0, t1, t2, t3, send_ref, x_ref):
    for a in range(x_ref.shape[0]):
        x = base_ref[0, a]
        image = base_ref[1, a] * x + summed(got_ref, a)
        x_ref[a] = (image - centre * x) * (sigma_first / half)
    mirror_products(codes, me[0], x_ref, (t0, t1, t2, t3), send_ref)


def third_kernel(codes, me, base_ref, last_ref, got_ref, t0, t1, t2, t3, send_ref, x_ref):
    for a in range(x_ref.shape[0]):
        x = last_ref[a]
        image = base_ref[1, a] * x + summed(got_ref, a)
        x_ref[a] = (image - centre * x) * (2.0 * sigma_next / half) - (
            sigma_first * sigma_next
        ) * base_ref[0, a]
    mirror_products(codes, me[0], x_ref, (t0, t1, t2, t3), send_ref)


def direct_kernel(codes, me, got_ref, t0, t1, t2, t3, send_ref, sums_ref):
    direct_products(codes, me[0], got_ref, (t0, t1, t2, t3), sums_ref)
    for peer in range(send_ref.shape[0]):
        send_ref[peer] = sums_ref[...]


def last_direct_kernel(codes, me, base_ref, x_ref, got_ref, t0, t1, t2, t3, send_ref, sums_ref):
    direct_products(codes, me[0], got_ref, (t0, t1, t2, t3), sums_ref)
    cols, vecs = sums_ref.shape[0], send_ref.shape[1] // 3
    halves = send_ref.shape[0] // cols
    x = x_ref[me[0]]
    energy = base_ref[1, me[0]]
    crossed = x_ref[0] * sums_ref[0]
    for a in range(1, cols):
        crossed = crossed + x_ref[a] * sums_ref[a]
    for z in range(halves):
        part = slice(z * vecs, (z + 1) * vecs)
        square = x[part] * x[part]
        local = crossed[part] + energy[part] * square
        for c in range(cols):
            send_ref[c * halves + z, :vecs, :] = sums_ref[c, part, :]
            send_ref[c * halves + z, vecs : 2 * vecs, :] = local
            send_ref[c * halves + z, 2 * vecs :, :] = square


def own_part(ref, index, half_index, vecs):
    block = ref[index]
    part = block[:vecs]
    for z in range(1, block.shape[0] // vecs):
        part = jnp.where(half_index == z, block[z * vecs : (z + 1) * vecs], part)
    return part


def image_kernel(got_ref, image_ref, send_ref):
    vecs = image_ref.shape[0]
    total = got_ref[0]
    for peer in range(1, got_ref.shape[0]):
        total = total + got_ref[peer]
    image_ref[...] = total[:vecs]
    for k in range(send_ref.shape[0]):
        send_ref[k] = total[vecs:]


def correct_kernel(me, base_ref, x_ref, image_ref, got_ref, out_ref, ritz_ref):
    vecs = out_ref.shape[0]
    total = got_ref[0]
    for k in range(1, got_ref.shape[0]):
        total = total + got_ref[k]
    total = jnp.sum(total, axis=1, keepdims=True)
    ritz = total[:vecs] / (total[vecs:] + 1e-06)
    x = own_part(x_ref, me[0], me[1], vecs)
    energy = base_ref[1, me[0]][:vecs]
    resid = energy * x + image_ref[...] - ritz * x
    spacing = energy - ritz
    out_ref[...] = x - spacing / jnp.maximum(spacing * spacing, 1.0) * resid
    row = jnp.broadcast_to(ritz[:1], (1, x.shape[1]))
    lane = lax.broadcasted_iota(jnp.int32, row.shape, 1)
    for v in range(1, vecs):
        row = jnp.where(lane == v, ritz[v : v + 1], row)
    ritz_ref[...] = row[:, :vecs]


def on_device(vectors, energies, tiles, tile_codes):
    rows = lax.axis_size(ROW)
    cols = lax.axis_size("col")
    halves = 1
    slots, side = tiles.shape[0], tiles.shape[1]
    vecs = vectors.shape[0]
    wide = vecs * halves
    first, stored, me = pl.pallas_call(
        prepare_kernel,
        out_shape=[
            jax.ShapeDtypeStruct((cols * halves, 2 * vecs, side), jnp.float32),
            pltpu.VMEM((slots + 1, side, side), tiles.dtype),
            pltpu.SMEM((2,), jnp.int32),
        ],
        in_specs=[SMEM] + [VMEM] * 3,
        out_specs=[VMEM, VMEM, SMEM],
    )(tile_codes, vectors, energies[None], tiles)
    first = exchange(first, COL)
    swap = [(0, 1), (1, 0)]
    far = lax.ppermute(stored, "z_hi", swap)
    near = lax.ppermute(stored, "core", swap)
    far, _ = lax.optimization_barrier((far, first))
    far_near = lax.ppermute(far, "core", swap)
    pair = (stored, near, far, far_near)

    row_shape = (rows, 2 * wide, side)
    state_shape = (cols, wide, side)
    col_shape = (cols * halves, cols, wide, side)
    send, base, codes = pl.pallas_call(
        start_kernel,
        out_shape=[
            pltpu.VMEM(row_shape, jnp.float32),
            pltpu.VMEM((2, *state_shape), jnp.float32),
            pltpu.SMEM((len(pair) * slots,), jnp.int32),
        ],
        in_specs=[SMEM] + [VMEM] * (1 + len(pair)),
        out_specs=[VMEM, VMEM, SMEM],
    )(
        pltpu.with_memory_space_constraint(me, pltpu.SMEM),
        *(pltpu.with_memory_space_constraint(a, pltpu.VMEM) for a in (first, *pair)),
    )
    scalars = (codes, me)

    def col_step(got):
        (send,) = call(direct_kernel, [col_shape], scalars, (got, *pair), [state_shape])
        return exchange(send, COL)

    got = col_step(exchange(send, ROW))
    send, x1 = call(second_kernel, [row_shape, state_shape], scalars, (base, got, *pair))
    got = col_step(exchange(send, ROW))
    send, x2 = call(third_kernel, [row_shape, state_shape], scalars, (base, x1, got, *pair))
    got = exchange(send, ROW)
    (send,) = call(
        last_direct_kernel,
        [(cols * halves, 3 * vecs, side)],
        scalars,
        (base, x2, got, *pair),
        [state_shape],
    )
    got = exchange(send, COL)
    image, send = call(image_kernel, [(vecs, side), (rows, 2 * vecs, side)], (), (got,))
    got = exchange(send, ROW)
    out, ritz = call(
        correct_kernel,
        [(vecs, side), (1, vecs)],
        (me,),
        (base, x2, image, got),
        space=jax.ShapeDtypeStruct,
    )
    return out, ritz[0]


def solution(mesh):
    split = Mesh(
        mesh.devices.reshape(6, 4, mesh.shape["col"], 2, 2),
        ("z_lo", "x", "col", "z_hi", "core"),
    )
    return jax.shard_map(
        on_device,
        mesh=split,
        in_specs=(P(REP, ROW_COL), P(ROW_COL), P(ROW_COL_REP, None, None), P(ROW_COL_REP)),
        out_specs=(P(REP, ROW_COL), P(REP)),
        check_vma=False,
    )
```

```python
import jax
import jax.numpy as jnp
from jax import lax
from jax.experimental import pallas as pl
from jax.experimental.pallas import tpu as pltpu
from jax.sharding import Mesh
from jax.sharding import PartitionSpec as P

ROW = ("z_lo", "x")
COL = "col"
REP = ("z_hi", "core")
ROW_COL = ("z_lo", "x", "col")
ROW_COL_REP = ("z_lo", "x", "col", "z_hi", "core")

filter_low = 5.0
filter_top = 20.0
spectrum_low = -3.0

half = (filter_top - filter_low) / 2.0
centre = (filter_top + filter_low) / 2.0
sigma_first = half / (spectrum_low - centre)
tau_value = 2.0 / sigma_first
sigma_next = 1.0 / (tau_value - sigma_first)

VMEM = pl.BlockSpec(memory_space=pltpu.VMEM)
SMEM = pl.BlockSpec(memory_space=pltpu.SMEM)
LABEL_ROWS = 16


def exchange(blocks, axis):
    return lax.all_to_all(blocks, axis, 0, 0, tiled=True)


def call(body, out_shapes, scalars, arrays, scratch=(), space=pltpu.VMEM):
    arrays = [pltpu.with_memory_space_constraint(a, pltpu.VMEM) for a in arrays]
    scalars = [pltpu.with_memory_space_constraint(a, pltpu.SMEM) for a in scalars]
    return pl.pallas_call(
        body,
        out_shape=[space(shape, jnp.float32) for shape in out_shapes],
        in_specs=[SMEM] * len(scalars) + [VMEM] * len(arrays),
        out_specs=[VMEM] * len(out_shapes),
        scratch_shapes=[pltpu.VMEM(shape, jnp.float32) for shape in scratch],
    )(*scalars, *arrays)


def place(code, rows):
    shift = 16
    a = (code * (-(-(1 << shift) // rows))) >> shift
    return a, code - a * rows


def slots_of(tile_refs):
    place_in_list = 0
    for tiles in tile_refs:
        side = tiles.shape[1]
        for slot in range(tiles.shape[0] // side):
            yield place_in_list, tiles.at[slot * side : (slot + 1) * side, :]
            place_in_list += 1


def mirror_products(codes, me, x_ref, tile_refs, send_ref):
    rows, vecs = send_ref.shape[0], x_ref.shape[1]
    own = x_ref[me]
    for k in range(rows):
        send_ref[k, :vecs, :] = jnp.zeros_like(own)
        send_ref[k, vecs:, :] = own
    for slot, tile in slots_of(tile_refs):
        a, k = place(codes[slot], rows)
        part = lax.dot_general(
            x_ref[a].astype(jnp.bfloat16),
            tile[...],
            (((1,), (0,)), ((), ())),
            preferred_element_type=jnp.float32,
        )
        send_ref[k, :vecs, :] += part


def direct_products(codes, me, got_ref, tile_refs, sums_ref):
    vecs = sums_ref.shape[1]
    rows = got_ref.shape[0]
    mirror = got_ref[0, :vecs, :]
    for k in range(1, rows):
        mirror = mirror + got_ref[k, :vecs, :]
    sums_ref[...] = jnp.zeros_like(sums_ref)
    sums_ref[me] = mirror
    for slot, tile in slots_of(tile_refs):
        a, k = place(codes[slot], rows)
        part = lax.dot_general(
            got_ref[k, vecs:, :].astype(jnp.bfloat16),
            tile[...],
            (((1,), (1,)), ((), ())),
            preferred_element_type=jnp.float32,
        )
        sums_ref[a] += part


def summed(got_ref, a):
    total = got_ref[0, a]
    for peer in range(1, got_ref.shape[0]):
        total = total + got_ref[peer, a]
    return total


def prepare_kernel(codes, vectors_ref, energies_ref, tiles_ref, send_ref, *refs):
    *part_refs, me = refs
    vecs = vectors_ref.shape[0]
    side = tiles_ref.shape[1]
    energy = jnp.broadcast_to(energies_ref[...], vectors_ref.shape)
    for peer in range(send_ref.shape[0]):
        send_ref[peer, :vecs, :] = vectors_ref[...]
        send_ref[peer, vecs:, :] = energy
    col_index = lax.axis_index("col")
    me[0] = col_index
    diagonal = col_index * lax.axis_size(ROW) + lax.axis_index(ROW)
    line = lax.broadcasted_iota(jnp.int32, (side, side), 0)
    lane = lax.broadcasted_iota(jnp.int32, (side, side), 1)
    last = part_refs[-1]
    label_rows = last.shape[0] % side
    label_lane = lax.broadcasted_iota(jnp.int32, (label_rows, side), 1)
    label = jnp.zeros((label_rows, side), jnp.float32)
    for slot, stored in slots_of(part_refs):
        code = codes[slot]
        bound = jnp.where(code < 0, -side, jnp.where(code == diagonal, 0, side))
        tile = tiles_ref[slot].astype(jnp.float32)
        stored[...] = jnp.where(line - lane < bound, tile, 0.0).astype(last.dtype)
        label = jnp.where(label_lane == slot, jnp.maximum(code, 0).astype(jnp.float32), label)
    last[last.shape[0] - label_rows :, :] = label.astype(last.dtype)


def start_kernel(me, first_ref, *refs):
    *tile_refs, send_ref, base_ref, codes = refs
    cols = base_ref.shape[1]
    halves = first_ref.shape[0] // cols
    vecs = first_ref.shape[1] // 2
    side = first_ref.shape[2]
    place_in_list = slots = 0
    for tiles in tile_refs:
        slots += tiles.shape[0] // side
        label_rows = tiles.shape[0] % side
        if label_rows:
            row = tiles[tiles.shape[0] - label_rows :, :].astype(jnp.float32)
            for slot in range(slots):
                codes[place_in_list + slot] = row[0, slot].astype(jnp.int32)
            place_in_list, slots = place_in_list + slots, 0
    for a in range(cols):
        for z in range(halves):
            part = slice(z * vecs, (z + 1) * vecs)
            base_ref[0, a, part, :] = first_ref[a * halves + z, :vecs, :]
            base_ref[1, a, part, :] = first_ref[a * halves + z, vecs:, :]
    mirror_products(codes, me[0], base_ref.at[0], tile_refs, send_ref)


def second_kernel(codes, me, base_ref, got_ref, *refs):
    *tile_refs, send_ref, x_ref = refs
    for a in range(x_ref.shape[0]):
        x = base_ref[0, a]
        image = base_ref[1, a] * x + summed(got_ref, a)
        x_ref[a] = (image - centre * x) * (sigma_first / half)
    mirror_products(codes, me[0], x_ref, tile_refs, send_ref)


def third_kernel(codes, me, base_ref, last_ref, got_ref, *refs):
    *tile_refs, send_ref, x_ref = refs
    for a in range(x_ref.shape[0]):
        x = last_ref[a]
        image = base_ref[1, a] * x + summed(got_ref, a)
        x_ref[a] = (image - centre * x) * (2.0 * sigma_next / half) - (
            sigma_first * sigma_next
        ) * base_ref[0, a]
    mirror_products(codes, me[0], x_ref, tile_refs, send_ref)


def direct_kernel(codes, me, got_ref, *refs):
    *tile_refs, send_ref, sums_ref = refs
    direct_products(codes, me[0], got_ref, tile_refs, sums_ref)
    for peer in range(send_ref.shape[0]):
        send_ref[peer] = sums_ref[...]


def last_direct_kernel(codes, me, base_ref, x_ref, got_ref, *refs):
    *tile_refs, send_ref, sums_ref = refs
    direct_products(codes, me[0], got_ref, tile_refs, sums_ref)
    cols, vecs = sums_ref.shape[0], send_ref.shape[1] // 3
    halves = send_ref.shape[0] // cols
    x = x_ref[me[0]]
    energy = base_ref[1, me[0]]
    crossed = x_ref[0] * sums_ref[0]
    for a in range(1, cols):
        crossed = crossed + x_ref[a] * sums_ref[a]
    for z in range(halves):
        part = slice(z * vecs, (z + 1) * vecs)
        square = x[part] * x[part]
        local = crossed[part] + energy[part] * square
        for c in range(cols):
            send_ref[c * halves + z, :vecs, :] = sums_ref[c, part, :]
            send_ref[c * halves + z, vecs : 2 * vecs, :] = local
            send_ref[c * halves + z, 2 * vecs :, :] = square


def image_kernel(got_ref, image_ref, send_ref):
    vecs = image_ref.shape[0]
    total = got_ref[0]
    for peer in range(1, got_ref.shape[0]):
        total = total + got_ref[peer]
    image_ref[...] = total[:vecs]
    for k in range(send_ref.shape[0]):
        send_ref[k] = total[vecs:]


def correct_kernel(me, base_ref, x_ref, image_ref, got_ref, out_ref, ritz_ref):
    vecs = out_ref.shape[0]
    total = got_ref[0]
    for k in range(1, got_ref.shape[0]):
        total = total + got_ref[k]
    total = jnp.sum(total, axis=1, keepdims=True)
    ritz = total[:vecs] / (total[vecs:] + 1e-06)
    x = x_ref[me[0]]
    energy = base_ref[1, me[0]]
    resid = energy * x + image_ref[...] - ritz * x
    spacing = energy - ritz
    out_ref[...] = x - spacing / jnp.maximum(spacing * spacing, 1.0) * resid
    row = jnp.broadcast_to(ritz[:1], (1, x.shape[1]))
    lane = lax.broadcasted_iota(jnp.int32, row.shape, 1)
    for v in range(1, vecs):
        row = jnp.where(lane == v, ritz[v : v + 1], row)
    ritz_ref[...] = row[:, :vecs]


def on_device(vectors, energies, tiles, tile_codes):
    rows = lax.axis_size(ROW)
    cols = lax.axis_size("col")
    halves = 1
    slots, side = tiles.shape[0], tiles.shape[1]
    vecs = vectors.shape[0]
    wide = vecs * halves
    early = slots // 2 + 1
    part_rows = (early * side, (slots - early) * side + LABEL_ROWS)
    first, *stored, me = pl.pallas_call(
        prepare_kernel,
        out_shape=[
            jax.ShapeDtypeStruct((cols * halves, 2 * vecs, side), jnp.float32),
            *(pltpu.VMEM((part, side), tiles.dtype) for part in part_rows),
            pltpu.SMEM((1,), jnp.int32),
        ],
        in_specs=[SMEM] + [VMEM] * 3,
        out_specs=[VMEM] * (1 + len(part_rows)) + [SMEM],
    )(tile_codes, vectors, energies[None], tiles)
    swap = [(0, 1), (1, 0)]
    far = []
    for part in stored:
        far.append(lax.ppermute(part, "z_hi", swap))
    first = exchange(first, COL)
    near = []
    for part in stored:
        near.append(lax.ppermute(part, "core", swap))
    far_near = []
    for part in far:
        part, _ = lax.optimization_barrier((part, first))
        far_near.append(lax.ppermute(part, "core", swap))
    pair = (*stored, *near, *far, *far_near)

    row_shape = (rows, 2 * wide, side)
    state_shape = (cols, wide, side)
    col_shape = (cols * halves, cols, wide, side)
    send, base, codes = pl.pallas_call(
        start_kernel,
        out_shape=[
            pltpu.VMEM(row_shape, jnp.float32),
            pltpu.VMEM((2, *state_shape), jnp.float32),
            pltpu.SMEM((4 * slots,), jnp.int32),
        ],
        in_specs=[SMEM] + [VMEM] * (1 + len(pair)),
        out_specs=[VMEM, VMEM, SMEM],
    )(
        pltpu.with_memory_space_constraint(me, pltpu.SMEM),
        *(pltpu.with_memory_space_constraint(a, pltpu.VMEM) for a in (first, *pair)),
    )
    scalars = (codes, me)

    def col_step(got):
        (send,) = call(direct_kernel, [col_shape], scalars, (got, *pair), [state_shape])
        return exchange(send, COL)

    got = col_step(exchange(send, ROW))
    send, x1 = call(second_kernel, [row_shape, state_shape], scalars, (base, got, *pair))
    got = col_step(exchange(send, ROW))
    send, x2 = call(third_kernel, [row_shape, state_shape], scalars, (base, x1, got, *pair))
    got = exchange(send, ROW)
    (send,) = call(
        last_direct_kernel,
        [(cols * halves, 3 * vecs, side)],
        scalars,
        (base, x2, got, *pair),
        [state_shape],
    )
    got = exchange(send, COL)
    image, send = call(image_kernel, [(vecs, side), (rows, 2 * vecs, side)], (), (got,))
    got = exchange(send, ROW)
    out, ritz = call(
        correct_kernel,
        [(vecs, side), (1, vecs)],
        (me,),
        (base, x2, image, got),
        space=jax.ShapeDtypeStruct,
    )
    return out, ritz[0]


def solution(mesh):
    split = Mesh(
        mesh.devices.reshape(6, 4, mesh.shape["col"], 2, 2),
        ("z_lo", "x", "col", "z_hi", "core"),
    )
    return jax.shard_map(
        on_device,
        mesh=split,
        in_specs=(P(REP, ROW_COL), P(ROW_COL), P(ROW_COL_REP, None, None), P(ROW_COL_REP)),
        out_specs=(P(REP, ROW_COL), P(REP)),
        check_vma=False,
    )
```

```python
import jax
import jax.numpy as jnp
from jax import lax
from jax.experimental import pallas as pl
from jax.experimental.pallas import tpu as pltpu
from jax.sharding import Mesh
from jax.sharding import PartitionSpec as P

ROW = ("z_lo", "x")
COL = "col"
REP = ("z_hi", "core")
ROW_COL = ("z_lo", "x", "col")
ROW_COL_REP = ("z_lo", "x", "col", "z_hi", "core")

filter_low = 5.0
filter_top = 20.0
spectrum_low = -3.0

half = (filter_top - filter_low) / 2.0
centre = (filter_top + filter_low) / 2.0
sigma_first = half / (spectrum_low - centre)
tau_value = 2.0 / sigma_first
sigma_next = 1.0 / (tau_value - sigma_first)

VMEM = pl.BlockSpec(memory_space=pltpu.VMEM)
SMEM = pl.BlockSpec(memory_space=pltpu.SMEM)
LABEL_ROWS = 16


def exchange(blocks, axis):
    return lax.all_to_all(blocks, axis, 0, 0, tiled=True)


def call(body, out_shapes, scalars, arrays, scratch=(), space=pltpu.VMEM):
    arrays = [pltpu.with_memory_space_constraint(a, pltpu.VMEM) for a in arrays]
    scalars = [pltpu.with_memory_space_constraint(a, pltpu.SMEM) for a in scalars]
    return pl.pallas_call(
        body,
        out_shape=[space(shape, jnp.float32) for shape in out_shapes],
        in_specs=[SMEM] * len(scalars) + [VMEM] * len(arrays),
        out_specs=[VMEM] * len(out_shapes),
        scratch_shapes=[pltpu.VMEM(shape, jnp.float32) for shape in scratch],
    )(*scalars, *arrays)


def place(code, rows):
    shift = 16
    a = (code * (-(-(1 << shift) // rows))) >> shift
    return a, code - a * rows


def slots_of(tile_refs):
    place_in_list = 0
    for tiles in tile_refs:
        side = tiles.shape[1]
        for slot in range(tiles.shape[0] // side):
            yield place_in_list, tiles.at[slot * side : (slot + 1) * side, :]
            place_in_list += 1


def mirror_products(codes, me, x_ref, tile_refs, send_ref):
    rows, vecs = send_ref.shape[0], x_ref.shape[1]
    own = x_ref[me]
    for k in range(rows):
        send_ref[k, :vecs, :] = jnp.zeros_like(own)
        send_ref[k, vecs:, :] = own
    for slot, tile in slots_of(tile_refs):
        a, k = place(codes[slot], rows)
        part = lax.dot_general(
            x_ref[a].astype(jnp.bfloat16),
            tile[...],
            (((1,), (0,)), ((), ())),
            preferred_element_type=jnp.float32,
        )
        send_ref[k, :vecs, :] += part


def direct_products(codes, me, got_ref, tile_refs, sums_ref):
    vecs = sums_ref.shape[1]
    rows = got_ref.shape[0]
    mirror = got_ref[0, :vecs, :]
    for k in range(1, rows):
        mirror = mirror + got_ref[k, :vecs, :]
    sums_ref[...] = jnp.zeros_like(sums_ref)
    sums_ref[me] = mirror
    for slot, tile in slots_of(tile_refs):
        a, k = place(codes[slot], rows)
        part = lax.dot_general(
            got_ref[k, vecs:, :].astype(jnp.bfloat16),
            tile[...],
            (((1,), (1,)), ((), ())),
            preferred_element_type=jnp.float32,
        )
        sums_ref[a] += part


def summed(got_ref, a):
    total = got_ref[0, a]
    for peer in range(1, got_ref.shape[0]):
        total = total + got_ref[peer, a]
    return total


def spread_kernel(vectors_ref, partner_ref, energies_ref, send_ref):
    vecs = vectors_ref.shape[0]
    energy = jnp.broadcast_to(energies_ref[...], vectors_ref.shape)
    for peer in range(send_ref.shape[0]):
        send_ref[peer, :vecs, :] = vectors_ref[...]
        send_ref[peer, vecs : 2 * vecs, :] = energy
        send_ref[peer, 2 * vecs :, :] = partner_ref[...]


def prepare_kernel(codes, tiles_ref, *refs):
    *part_refs, me = refs
    side = tiles_ref.shape[1]
    col_index = lax.axis_index("col")
    me[0] = col_index
    me[1] = lax.axis_index("z_hi")
    diagonal = col_index * lax.axis_size(ROW) + lax.axis_index(ROW)
    line = lax.broadcasted_iota(jnp.int32, (side, side), 0)
    lane = lax.broadcasted_iota(jnp.int32, (side, side), 1)
    last = part_refs[-1]
    label_rows = last.shape[0] % side
    label_lane = lax.broadcasted_iota(jnp.int32, (label_rows, side), 1)
    label = jnp.zeros((label_rows, side), jnp.float32)
    for slot, stored in slots_of(part_refs):
        code = codes[slot]
        bound = jnp.where(code < 0, -side, jnp.where(code == diagonal, 0, side))
        tile = tiles_ref[slot].astype(jnp.float32)
        stored[...] = jnp.where(line - lane < bound, tile, 0.0).astype(last.dtype)
        label = jnp.where(label_lane == slot, jnp.maximum(code, 0).astype(jnp.float32), label)
    last[last.shape[0] - label_rows :, :] = label.astype(last.dtype)


def read_codes(tile_refs, codes):
    place_in_list = slots = 0
    for tiles in tile_refs:
        side = tiles.shape[1]
        slots += tiles.shape[0] // side
        label_rows = tiles.shape[0] % side
        if label_rows:
            row = tiles[tiles.shape[0] - label_rows :, :].astype(jnp.float32)
            for slot in range(slots):
                codes[place_in_list + slot] = row[0, slot].astype(jnp.int32)
            place_in_list, slots = place_in_list + slots, 0


def start_kernel(me, first_ref, *refs):
    *tile_refs, send_ref, base_ref, codes, x_ref = refs
    read_codes(tile_refs, codes)
    cols, vecs = base_ref.shape[1], base_ref.shape[2]
    halves = x_ref.shape[1] // vecs
    rows = send_ref.shape[0] // halves
    for a in range(cols):
        base_ref[0, a] = first_ref[a, :vecs, :]
        base_ref[1, a] = first_ref[a, vecs : 2 * vecs, :]
        x_ref[a, :vecs, :] = first_ref[a, :vecs, :]
        x_ref[a, vecs:, :] = first_ref[a, 2 * vecs :, :]
    own = base_ref[0, me[0]]
    for peer in range(send_ref.shape[0]):
        send_ref[peer, :vecs, :] = jnp.zeros_like(own)
        send_ref[peer, vecs:, :] = own
    for slot, tile in slots_of(tile_refs):
        a, k = place(codes[slot], rows)
        part = lax.dot_general(
            x_ref[a].astype(jnp.bfloat16),
            tile[...],
            (((1,), (0,)), ((), ())),
            preferred_element_type=jnp.float32,
        )
        send_ref[k * halves + me[1], :vecs, :] += part[:vecs]
        send_ref[k * halves + 1 - me[1], :vecs, :] += part[vecs:]


def first_direct_kernel(me, got_ref, *refs):
    *tile_refs, send_ref, codes, sums_ref, mine_ref = refs
    read_codes(tile_refs, codes)
    rows, vecs = mine_ref.shape[0], sums_ref.shape[1]
    halves = got_ref.shape[0] // rows
    for k in range(rows):
        mirror = got_ref[k * halves, :vecs, :]
        for z in range(1, halves):
            mirror = mirror + got_ref[k * halves + z, :vecs, :]
        mine_ref[k, :vecs, :] = mirror
        mine_ref[k, vecs:, :] = got_ref[k * halves + me[1], vecs:, :]
    direct_products(codes, me[0], mine_ref, tile_refs, sums_ref)
    for peer in range(send_ref.shape[0]):
        send_ref[peer] = sums_ref[...]


def second_kernel(codes, me, base_ref, got_ref, *refs):
    *tile_refs, send_ref, x_ref = refs
    for a in range(x_ref.shape[0]):
        x = base_ref[0, a]
        image = base_ref[1, a] * x + summed(got_ref, a)
        x_ref[a] = (image - centre * x) * (sigma_first / half)
    mirror_products(codes, me[0], x_ref, tile_refs, send_ref)


def third_kernel(codes, me, base_ref, last_ref, got_ref, *refs):
    *tile_refs, send_ref, x_ref = refs
    for a in range(x_ref.shape[0]):
        x = last_ref[a]
        image = base_ref[1, a] * x + summed(got_ref, a)
        x_ref[a] = (image - centre * x) * (2.0 * sigma_next / half) - (
            sigma_first * sigma_next
        ) * base_ref[0, a]
    mirror_products(codes, me[0], x_ref, tile_refs, send_ref)


def direct_kernel(codes, me, got_ref, *refs):
    *tile_refs, send_ref, sums_ref = refs
    direct_products(codes, me[0], got_ref, tile_refs, sums_ref)
    for peer in range(send_ref.shape[0]):
        send_ref[peer] = sums_ref[...]


def last_direct_kernel(codes, me, base_ref, x_ref, got_ref, *refs):
    *tile_refs, send_ref, sums_ref = refs
    direct_products(codes, me[0], got_ref, tile_refs, sums_ref)
    cols, vecs = sums_ref.shape[0], send_ref.shape[1] // 3
    halves = send_ref.shape[0] // cols
    x = x_ref[me[0]]
    energy = base_ref[1, me[0]]
    crossed = x_ref[0] * sums_ref[0]
    for a in range(1, cols):
        crossed = crossed + x_ref[a] * sums_ref[a]
    for z in range(halves):
        part = slice(z * vecs, (z + 1) * vecs)
        square = x[part] * x[part]
        local = crossed[part] + energy[part] * square
        for c in range(cols):
            send_ref[c * halves + z, :vecs, :] = sums_ref[c, part, :]
            send_ref[c * halves + z, vecs : 2 * vecs, :] = local
            send_ref[c * halves + z, 2 * vecs :, :] = square


def image_kernel(got_ref, image_ref, send_ref):
    vecs = image_ref.shape[0]
    total = got_ref[0]
    for peer in range(1, got_ref.shape[0]):
        total = total + got_ref[peer]
    image_ref[...] = total[:vecs]
    for k in range(send_ref.shape[0]):
        send_ref[k] = total[vecs:]


def correct_kernel(me, base_ref, x_ref, image_ref, got_ref, out_ref, ritz_ref):
    vecs = out_ref.shape[0]
    total = got_ref[0]
    for k in range(1, got_ref.shape[0]):
        total = total + got_ref[k]
    total = jnp.sum(total, axis=1, keepdims=True)
    ritz = total[:vecs] / (total[vecs:] + 1e-06)
    x = x_ref[me[0]]
    energy = base_ref[1, me[0]]
    resid = energy * x + image_ref[...] - ritz * x
    spacing = energy - ritz
    out_ref[...] = x - spacing / jnp.maximum(spacing * spacing, 1.0) * resid
    row = jnp.broadcast_to(ritz[:1], (1, x.shape[1]))
    lane = lax.broadcasted_iota(jnp.int32, row.shape, 1)
    for v in range(1, vecs):
        row = jnp.where(lane == v, ritz[v : v + 1], row)
    ritz_ref[...] = row[:, :vecs]


def on_device(vectors, energies, tiles, tile_codes):
    rows = lax.axis_size(ROW)
    cols = lax.axis_size("col")
    slots, side = tiles.shape[0], tiles.shape[1]
    vecs = vectors.shape[0]
    early = slots * 3 // 4
    part_rows = (early * side, (slots - early) * side + LABEL_ROWS)
    swap = [(0, 1), (1, 0)]
    partner = lax.ppermute(vectors, "z_hi", swap)
    *stored, me = pl.pallas_call(
        prepare_kernel,
        out_shape=[
            *(pltpu.VMEM((part, side), tiles.dtype) for part in part_rows),
            pltpu.SMEM((2,), jnp.int32),
        ],
        in_specs=[SMEM, VMEM],
        out_specs=[VMEM] * len(part_rows) + [SMEM],
    )(tile_codes, tiles)
    far = []
    for part in stored:
        far.append(lax.ppermute(part, "z_hi", swap))
    near = []
    for part in stored:
        near.append(lax.ppermute(part, "core", swap))
    first = pl.pallas_call(
        spread_kernel,
        out_shape=jax.ShapeDtypeStruct((cols, 3 * vecs, side), jnp.float32),
        in_specs=[VMEM] * 3,
        out_specs=VMEM,
    )(vectors, pltpu.with_memory_space_constraint(partner, pltpu.VMEM), energies[None])
    first = exchange(first, COL)

    row_shape = (rows, 2 * vecs, side)
    state_shape = (cols, vecs, side)
    col_shape = (cols, cols, vecs, side)
    halves = lax.axis_size("z_hi")

    def held(*arrays):
        return [pltpu.with_memory_space_constraint(a, pltpu.VMEM) for a in arrays]

    chip = (*stored, *near)
    me = pltpu.with_memory_space_constraint(me, pltpu.SMEM)
    send, base = pl.pallas_call(
        start_kernel,
        out_shape=[
            pltpu.VMEM((rows * halves, 2 * vecs, side), jnp.float32),
            pltpu.VMEM((2, *state_shape), jnp.float32),
        ],
        in_specs=[SMEM] + [VMEM] * (1 + len(chip)),
        out_specs=[VMEM, VMEM],
        scratch_shapes=[
            pltpu.SMEM((2 * slots,), jnp.int32),
            pltpu.VMEM((cols, halves * vecs, side), jnp.float32),
        ],
    )(me, *held(first, *chip))
    far_near = []
    for part in far:
        part, _ = lax.optimization_barrier((part, base))
        far_near.append(lax.ppermute(part, "core", swap))
    pair = (*chip, *far, *far_near)
    got = exchange(send, (*ROW, "z_hi"))
    send, codes = pl.pallas_call(
        first_direct_kernel,
        out_shape=[pltpu.VMEM(col_shape, jnp.float32), pltpu.SMEM((4 * slots,), jnp.int32)],
        in_specs=[SMEM] + [VMEM] * (1 + len(pair)),
        out_specs=[VMEM, SMEM],
        scratch_shapes=[
            pltpu.VMEM(state_shape, jnp.float32),
            pltpu.VMEM(row_shape, jnp.float32),
        ],
    )(me, *held(got, *pair))
    got = exchange(send, COL)
    scalars = (codes, me)

    def col_step(got):
        (send,) = call(direct_kernel, [col_shape], scalars, (got, *pair), [state_shape])
        return exchange(send, COL)

    send, x1 = call(second_kernel, [row_shape, state_shape], scalars, (base, got, *pair))
    got = col_step(exchange(send, ROW))
    send, x2 = call(third_kernel, [row_shape, state_shape], scalars, (base, x1, got, *pair))
    got = exchange(send, ROW)
    (send,) = call(
        last_direct_kernel,
        [(cols, 3 * vecs, side)],
        scalars,
        (base, x2, got, *pair),
        [state_shape],
    )
    got = exchange(send, COL)
    image, send = call(image_kernel, [(vecs, side), (rows, 2 * vecs, side)], (), (got,))
    got = exchange(send, ROW)
    out, ritz = call(
        correct_kernel,
        [(vecs, side), (1, vecs)],
        (me,),
        (base, x2, image, got),
        space=jax.ShapeDtypeStruct,
    )
    return out, ritz[0]


def solution(mesh):
    split = Mesh(
        mesh.devices.reshape(6, 4, mesh.shape["col"], 2, 2),
        ("z_lo", "x", "col", "z_hi", "core"),
    )
    return jax.shard_map(
        on_device,
        mesh=split,
        in_specs=(P(REP, ROW_COL), P(ROW_COL), P(ROW_COL_REP, None, None), P(ROW_COL_REP)),
        out_specs=(P(REP, ROW_COL), P(REP)),
        check_vma=False,
    )
```
